32 devices in a mesh: depth: 8 (over z, y), xline: 4 (over x, core).
Axes of the slice: x: 2, y: 2, z: 4, core: 2. Of those that a mesh axis runs over, the one named last changes fastest.
Arguments:
- surface_fields: float32 [2, 2, 2, 64, 128], P(None, None, None, 'xline'), may hold values from -6 to 6
- stencil_table: float32 [13, 2, 2, 128], replicated
- velocity_bins: int32 [8, 2, 64, 128], P('depth', None, 'xline'), may hold values from 0 to 127
- offset_list: int32 [16, 2], replicated, may hold values from -8 to 8, as said below
Outputs:
- image_tiles: float32 [8, 16, 64, 128], P('depth', None, 'xline')
The draws below stay inside these ranges and needn't reach their ends.
Inputs may be any that keep to these rules, and one draw needn't show every extreme that they name: `offset_list`: column 0 lies within -8 to 8 and column 1 within -8 to 8; both ends of both ranges occur in every draw.
All inputs are finite; a program needn't handle non-finite values.
Results may differ from the reference program's by a relative error of at most 0.0003.
Values sent between devices are 32-bit elements; how exact they have to be, the bound alone decides.
No kernel may reach another device: no remote copies, remote signals or barrier semaphores. Data moves between devices by JAX's collectives and lax.ppermute only.
A program may use at most 64 MiB of HBM per device.

```python
import jax
import jax.numpy as jnp
from jax import lax

NXI = 128
F = 2
LEVELS = 2
TAPS = 13
NVEL = 128
OFFS = 16
OFF_Y = 8
OFF_X = 8
SLABS = 8
CROSS = 64


def draw_stencil_table(key, part):
    subkeys = jax.random.split(key, 5)
    share_freq = 0.1 * 2.5 ** jax.random.uniform(subkeys[0], (F,))
    bin_ids = jnp.arange(NVEL, dtype=jnp.float32)
    factor = 0.5 * 4.0 ** (bin_ids / NVEL)
    shares = jnp.minimum(share_freq[:, None] * factor[None, :], 0.5)
    salt_share = jax.random.uniform(subkeys[1], (F, NVEL), minval=0.3, maxval=0.6)
    shares = jnp.where(bin_ids[None, :] >= NVEL - 16, salt_share, shares)
    raw_weights = jax.random.uniform(subkeys[2], (TAPS - 1, F, NVEL), minval=0.5, maxval=1.5)
    neighbour = jnp.sqrt(shares[None] * raw_weights / jnp.sum(raw_weights, axis=0, keepdims=True))
    weights = jnp.concatenate([jnp.sqrt(1.0 - shares)[None], neighbour], axis=0)
    base_phase = jax.random.uniform(subkeys[3], (1, F, NVEL), minval=-jnp.pi, maxval=jnp.pi)
    jitter = jax.random.uniform(subkeys[4], (TAPS, F, NVEL), minval=-0.5, maxval=0.5)
    jitter = jitter.at[0].set(0.0)
    phases = base_phase + jitter
    return jnp.stack([weights * jnp.cos(phases), weights * jnp.sin(phases)], axis=1).astype(jnp.float32)


def draw_velocity_bins(key, part):
    subkeys = jax.random.split(key, 4)
    chain_levels = SLABS * LEVELS
    sorted_positions = jax.random.permutation(subkeys[3], chain_levels)
    base_bins = jax.random.randint(subkeys[0], (chain_levels, 1, 1), 0, NVEL - 63)
    base_bins = jnp.where((sorted_positions == 2)[:, None, None], 0, base_bins)
    cell_velocity_groups = base_bins + jax.random.randint(subkeys[1], (chain_levels, CROSS, NXI), 0, 48)
    salt_velocity_groups = NVEL - 16 + jax.random.randint(subkeys[2], (chain_levels, CROSS, NXI), 0, 16)
    sudden_spike = (sorted_positions < 2)[:, None, None]
    selected_entry = jnp.where(sudden_spike, salt_velocity_groups, cell_velocity_groups)
    return selected_entry.reshape(SLABS, LEVELS, CROSS, NXI).astype(jnp.int32)


def draw_offset_list(key, part):
    subkeys = jax.random.split(key, 3)
    cross_shift = jax.random.randint(subkeys[0], (OFFS,), -OFF_Y, OFF_Y + 1)
    inline_shift = jax.random.randint(subkeys[1], (OFFS,), -OFF_X, OFF_X + 1)
    cross_shift = cross_shift.at[0].set(-OFF_Y).at[1].set(OFF_Y)
    inline_shift = inline_shift.at[2].set(-OFF_X).at[3].set(OFF_X)
    pairs = jnp.stack([cross_shift, inline_shift], axis=1)
    return pairs[jax.random.permutation(subkeys[2], OFFS)].astype(jnp.int32)


def steps_of(key, dims, cuts, smallest, largest):
    def one(position, shards_of):
        draws = jax.random.uniform(jax.random.fold_in(jax.random.fold_in(key, 6), position), (shards_of,), jnp.float32, smallest / len(cuts), largest / len(cuts))
        return jnp.repeat(jnp.exp(draws), dims[position] // shards_of).reshape((-1,) + (1,) * (len(dims) - position - 1))

    loudness = one(*cuts[0])
    for cut in cuts[1:]:
        loudness = loudness * one(*cut)
    return loudness


def gaussian(own_key, extent, width, reach, cuts=(), kind=jnp.bfloat16):
    result = jax.random.normal(own_key, extent, jnp.float32) * width
    if len(cuts) > 0:
        result = steps_of(own_key, extent, cuts, -0.22, 0.18) * result
    return jnp.clip(result, min=-reach, max=reach).astype(kind)


def setup_inputs(seed: int = 0) -> dict:
    splits = jax.random.split(jax.random.key(seed), 5)
    surface_fields = gaussian(splits[0], (2, 2, F, CROSS, NXI), 1.0, 6.0, ((3, 4),), jnp.float32)
    stencil_table = draw_stencil_table(jax.random.fold_in(splits[4], 71), 0)
    velocity_bins = draw_velocity_bins(jax.random.fold_in(splits[4], 71), 0)
    offset_list = draw_offset_list(jax.random.fold_in(splits[4], 71), 0)
    return {"surface_fields": surface_fields, "stencil_table": stencil_table, "velocity_bins": velocity_bins, "offset_list": offset_list}


tap_rows = (0, -4, -3, -2, -1, 1, 2, 3, 4, 0, 0, 0, 0)
tap_cols = (0, 0, 0, 0, 0, 0, 0, 0, 0, -2, -1, 1, 2)
reach_rows = 4
reach_cols = 2


def extrapolate(fields, coefficients):
    row_count = fields.shape[3] - 2 * reach_rows
    inline_width = fields.shape[4]
    padded = jnp.pad(fields, ((0, 0), (0, 0), (0, 0), (0, 0), (reach_cols, reach_cols)))
    conj_sign = jnp.array([1.0, -1.0], dtype=fields.dtype).reshape(2, 1, 1, 1)
    real_part = None
    imag_part = None
    for tap_index in range(len(tap_rows)):
        first_row = reach_rows + tap_rows[tap_index]
        first_col = reach_cols + tap_cols[tap_index]
        shifted = padded[:, :, :, first_row:first_row + row_count, first_col:first_col + inline_width]
        coef_real = coefficients[tap_index, 0]
        coef_imag = coefficients[tap_index, 1] * conj_sign
        term_real = coef_real * shifted[:, 0] - coef_imag * shifted[:, 1]
        term_imag = coef_real * shifted[:, 1] + coef_imag * shifted[:, 0]
        if tap_index == 0:
            real_part = term_real
            imag_part = term_imag
        else:
            real_part = real_part + term_real
            imag_part = imag_part + term_imag
    return jnp.stack([real_part, imag_part], axis=1)


def correlate(fields, offset_list):
    source = fields[0]
    receiver = fields[1]
    padded = jnp.pad(receiver, ((0, 0), (0, 0), (OFF_Y, OFF_Y), (OFF_X, OFF_X)))
    slice_shape = (2, source.shape[1], source.shape[2], source.shape[3])

    def one_offset(offset_couple):
        starts = (jnp.int32(0), jnp.int32(0), OFF_Y + offset_couple[0], OFF_X + offset_couple[1])
        shifted = lax.dynamic_slice(padded, starts, slice_shape)
        return jnp.sum(source[0] * shifted[0] + source[1] * shifted[1], axis=0)

    return lax.map(one_offset, offset_list)


def reference(surface_fields, stencil_table, velocity_bins, offset_list):
    def slab_step(fields, slab_velocity):
        for level_index in range(LEVELS):
            coefficients = jnp.take(stencil_table, slab_velocity[level_index], axis=3)
            padded = jnp.pad(fields, ((0, 0), (0, 0), (0, 0), (reach_rows, reach_rows), (0, 0)))
            fields = extrapolate(padded, coefficients)
        return fields, correlate(fields, offset_list)

    final_fields, images = lax.scan(slab_step, surface_fields, velocity_bins)
    return images
```

```python
import functools

import jax
import jax.numpy as jnp
from jax import lax
from jax.experimental import pallas as pl
from jax.experimental.pallas import tpu as pltpu
from jax.sharding import PartitionSpec as P

OFF_Y = 8
OFF_X = 8
TAP_ROWS = (0, -4, -3, -2, -1, 1, 2, 3, 4, 0, 0, 0, 0)
TAP_COLS = (0, 0, 0, 0, 0, 0, 0, 0, 0, -2, -1, 1, 2)
PAD = 8
SUB = 8


def swap(block, axis, bit):
    count = lax.axis_size(axis)
    return lax.ppermute(block, axis, [(i, i ^ bit) for i in range(count)])


def bits_of(count):
    return [1 << k for k in reversed(range(count.bit_length() - 1))]


def reversed_bits(value, count):
    width = count.bit_length() - 1
    total = 0
    for k in range(width):
        total = total + (((value >> k) & 1) << (width - 1 - k))
    return total


def image_kernel(
    sizes, offsets, table, surf_own, surf_other, bins_own, bins_other, image, wide, first, second
):
    depth_count, line_count, levels, row_count, freq_count, row_chunk = sizes
    depth_index = lax.axis_index("depth")
    line_index = lax.axis_index("xline")
    width = image.shape[3]
    grid_rows = row_count * line_count
    taps = len(TAP_ROWS)
    near_count = line_count // 2

    for row in range(table.shape[0]):
        wide[row] = jnp.broadcast_to(table[row : row + 1, :], (SUB, width))

    zeros = jnp.zeros((PAD, width), jnp.float32)
    for array in range(4 * freq_count):
        for buffer in (first, second):
            buffer[array, 0:PAD, :] = zeros
            buffer[array, PAD + grid_rows : 2 * PAD + grid_rows, :] = zeros

    for slot in range(near_count):
        for own, source in ((0, surf_own), (1, surf_other)):
            line = line_index ^ (2 * reversed_bits(slot, near_count) + own)
            start = pl.multiple_of(PAD + line * row_count, SUB)
            for array in range(4 * freq_count):
                block = source[slot, array]
                if array >= 3 * freq_count:
                    block = -block
                first[array, pl.ds(start, row_count), :] = block

    lane = lax.broadcasted_iota(jnp.int32, (SUB, width), 1)
    inside = {
        step: (lane + step >= 0) & (lane + step < width) for step in sorted(set(TAP_COLS) - {0})
    }

    def level(slab_slot, level_index, source, target):
        def chunk_step(chunk, carry):
            for block in range(row_chunk // SUB):
                row = pl.multiple_of(chunk * row_chunk + block * SUB, SUB)
                line = (row // row_count) ^ line_index
                slot = reversed_bits(line // 2, near_count)
                inner = pl.multiple_of(row % row_count, SUB)
                own = bins_own[slot, slab_slot, level_index, pl.ds(inner, SUB), :]
                other = bins_other[slot, slab_slot, level_index, pl.ds(inner, SUB), :]
                bins = jnp.where((line & 1) == 0, own, other)
                for freq in range(freq_count):
                    sums = [None] * 4
                    centre = None
                    for tap in range(taps):
                        coefs = [
                            jnp.take_along_axis(
                                wide[(tap * 2 + part) * freq_count + freq],
                                bins,
                                axis=1,
                                mode="promise_in_bounds",
                            )
                            for part in range(2)
                        ]
                        step = TAP_COLS[tap]
                        if step == 0:
                            fields = [
                                source[
                                    array * freq_count + freq,
                                    pl.ds(PAD + row + TAP_ROWS[tap], SUB),
                                    :,
                                ]
                                for array in range(4)
                            ]
                            if tap == 0:
                                centre = fields
                        else:
                            fields = [
                                jnp.where(
                                    inside[step], pltpu.roll(value, (-step) % width, 1), 0.0
                                )
                                for value in centre
                            ]
                        for field in range(2):
                            real, imag = fields[2 * field], fields[2 * field + 1]
                            term_real = coefs[0] * real - coefs[1] * imag
                            term_imag = coefs[0] * imag + coefs[1] * real
                            for part, term in ((0, term_real), (1, term_imag)):
                                place = 2 * field + part
                                sums[place] = term if sums[place] is None else sums[place] + term
                    for array in range(4):
                        target[array * freq_count + freq, pl.ds(PAD + row, SUB), :] = sums[array]
            return carry

        lax.fori_loop(0, grid_rows // row_chunk, chunk_step, 0)

    def slab_step(slab, carry):
        slot = reversed_bits(slab ^ depth_index, depth_count)
        buffers = (first, second)
        for level_index in range(levels):
            level(slot, level_index, buffers[level_index % 2], buffers[1 - level_index % 2])
        if levels % 2:
            first[...] = second[...]
        return carry

    lax.fori_loop(0, depth_index + 1, slab_step, 0)

    base = pl.multiple_of(PAD + line_index * row_count, SUB)
    lanes = lax.broadcasted_iota(jnp.int32, (row_count, width), 1)
    sources = [first[array, pl.ds(base, row_count), :] for array in range(2 * freq_count)]

    for h in range(image.shape[1]):
        dy = offsets[h, 0]
        dx = offsets[h, 1]
        valid = (lanes + dx >= 0) & (lanes + dx < width)
        total = None
        for array in range(2 * freq_count):
            value = first[2 * freq_count + array, pl.ds(base + dy, row_count), :]
            term = sources[array] * pltpu.roll(value, lax.rem(width - dx, width), 1)
            if array >= freq_count:
                term = -term
            total = term if total is None else total + term
        image[0, h] = jnp.where(valid, total, 0.0)


def shards(surface_fields, stencil_table, velocity_bins, offset_list):
    depth_count = lax.axis_size("depth")
    line_count = lax.axis_size("xline")
    row_count = surface_fields.shape[3]
    width = surface_fields.shape[4]
    freq_count = surface_fields.shape[2]
    levels = velocity_bins.shape[1]
    grid_rows = row_count * line_count
    row_chunk = next(rows for rows in (64, 32, 16, 8) if grid_rows % rows == 0)

    surf = surface_fields.reshape(1, 4 * freq_count, row_count, width)
    bins = velocity_bins
    line_bits = bits_of(line_count)[:-1]
    for bit in line_bits:
        surf = jnp.concatenate([surf, swap(surf, "xline", bit)], axis=0)
    for bit in bits_of(depth_count):
        bins = jnp.concatenate([bins, swap(bins, "depth", bit)], axis=0)
    bins = bins[None]
    for bit in line_bits:
        bins = jnp.concatenate([bins, swap(bins, "xline", bit)], axis=0)
    surf_other = swap(surf, "xline", 1)
    bins_other = swap(bins, "xline", 1)

    table = stencil_table.reshape(-1, stencil_table.shape[3])
    sizes = (depth_count, line_count, levels, row_count, freq_count, row_chunk)
    field_shape = (4 * freq_count, grid_rows + 2 * PAD, width)
    whole = pl.BlockSpec(memory_space=pltpu.VMEM)
    return pl.pallas_call(
        functools.partial(image_kernel, sizes),
        out_shape=jax.ShapeDtypeStruct((1, offset_list.shape[0], row_count, width), jnp.float32),
        in_specs=[pl.BlockSpec(memory_space=pltpu.SMEM)] + [whole] * 5,
        out_specs=whole,
        scratch_shapes=[
            pltpu.VMEM((table.shape[0], SUB, width), jnp.float32),
            pltpu.VMEM(field_shape, jnp.float32),
            pltpu.VMEM(field_shape, jnp.float32),
        ],
        name="continuation",
    )(offset_list, table, surf, surf_other, bins, bins_other)


def solution(mesh):
    return jax.shard_map(
        shards,
        mesh=mesh,
        in_specs=(P(None, None, None, "xline", None), P(), P("depth", None, "xline", None), P()),
        out_specs=P("depth", None, "xline", None),
        check_vma=False,
    )
```

```python
import functools

import jax
import jax.numpy as jnp
from jax import lax
from jax.experimental import pallas as pl
from jax.experimental.pallas import tpu as pltpu
from jax.sharding import PartitionSpec as P

OFF_Y = 8
OFF_X = 8
TAP_ROWS = (0, -4, -3, -2, -1, 1, 2, 3, 4, 0, 0, 0, 0)
TAP_COLS = (0, 0, 0, 0, 0, 0, 0, 0, 0, -2, -1, 1, 2)
PAD = 8
SUB = 8


def swap(block, axis, bit):
    count = lax.axis_size(axis)
    return lax.ppermute(block, axis, [(i, i ^ bit) for i in range(count)])


def bits_of(count):
    return [1 << k for k in reversed(range(count.bit_length() - 1))]


def reversed_bits(value, count):
    width = count.bit_length() - 1
    total = 0
    for k in range(width):
        total = total + (((value >> k) & 1) << (width - 1 - k))
    return total


def continuation_kernel(
    sizes, table, surf_own, surf_other, bins_own, bins_other, mine, theirs, wide, first, second
):
    depth_count, line_count, levels, row_count, freqs, row_chunk = sizes
    depth_index = lax.axis_index("depth")
    line_index = lax.axis_index("xline")
    parity = line_index & 1
    width = mine.shape[1]
    grid_rows = row_count * line_count
    taps = len(TAP_ROWS)
    near_count = line_count // 2

    for tap in range(taps):
        for part in range(2):
            for freq in range(freqs):
                row = table[tap, part, pl.ds(parity * freqs + freq, 1), :]
                wide[(tap * 2 + part) * freqs + freq] = jnp.broadcast_to(row, (SUB, width))

    zeros = jnp.zeros((PAD, width), jnp.float32)
    for array in range(4 * freqs):
        for buffer in (first, second):
            buffer[array, 0:PAD, :] = zeros
            buffer[array, PAD + grid_rows : 2 * PAD + grid_rows, :] = zeros

    for slot in range(near_count):
        for own, source in ((0, surf_own), (1, surf_other)):
            line = line_index ^ (2 * reversed_bits(slot, near_count) + own)
            start = pl.multiple_of(PAD + line * row_count, SUB)
            for kind in range(4):
                for freq in range(freqs):
                    block = source[slot, kind, parity * freqs + freq]
                    if kind == 3:
                        block = -block
                    first[kind * freqs + freq, pl.ds(start, row_count), :] = block

    lane = lax.broadcasted_iota(jnp.int32, (SUB, width), 1)
    inside = {
        step: (lane + step >= 0) & (lane + step < width) for step in sorted(set(TAP_COLS) - {0})
    }

    def level(slab_slot, level_index, source, target):
        def chunk_step(chunk, carry):
            for block in range(row_chunk // SUB):
                row = pl.multiple_of(chunk * row_chunk + block * SUB, SUB)
                line = (row // row_count) ^ line_index
                slot = reversed_bits(line // 2, near_count)
                inner = pl.multiple_of(row % row_count, SUB)
                own = bins_own[slot, slab_slot, level_index, pl.ds(inner, SUB), :]
                other = bins_other[slot, slab_slot, level_index, pl.ds(inner, SUB), :]
                bins = jnp.where((line & 1) == 0, own, other)
                for freq in range(freqs):
                    sums = [None] * 4
                    centre = None
                    for tap in range(taps):
                        coefs = [
                            jnp.take_along_axis(
                                wide[(tap * 2 + part) * freqs + freq],
                                bins,
                                axis=1,
                                mode="promise_in_bounds",
                            )
                            for part in range(2)
                        ]
                        step = TAP_COLS[tap]
                        if step == 0:
                            fields = [
                                source[kind * freqs + freq, pl.ds(PAD + row + TAP_ROWS[tap], SUB), :]
                                for kind in range(4)
                            ]
                            if tap == 0:
                                centre = fields
                        else:
                            fields = [
                                jnp.where(
                                    inside[step], pltpu.roll(value, (-step) % width, 1), 0.0
                                )
                                for value in centre
                            ]
                        for field in range(2):
                            real, imag = fields[2 * field], fields[2 * field + 1]
                            term_real = coefs[0] * real - coefs[1] * imag
                            term_imag = coefs[0] * imag + coefs[1] * real
                            for part, term in ((0, term_real), (1, term_imag)):
                                place = 2 * field + part
                                sums[place] = term if sums[place] is None else sums[place] + term
                    for kind in range(4):
                        target[kind * freqs + freq, pl.ds(PAD + row, SUB), :] = sums[kind]
            return carry

        lax.fori_loop(0, grid_rows // row_chunk, chunk_step, 0)

    def slab_step(slab, carry):
        slot = reversed_bits(slab ^ depth_index, depth_count)
        buffers = (first, second)
        for level_index in range(levels):
            level(slot, level_index, buffers[level_index % 2], buffers[1 - level_index % 2])
        if levels % 2:
            first[...] = second[...]
        return carry

    lax.fori_loop(0, depth_index + 1, slab_step, 0)

    tall = row_count + 2 * OFF_Y
    for out, line in ((mine, line_index), (theirs, line_index ^ 1)):
        base = pl.multiple_of(PAD + line * row_count, SUB)
        for array in range(2 * freqs):
            out[array * row_count : (array + 1) * row_count, :] = first[
                array, pl.ds(base, row_count), :
            ]
            start = 2 * freqs * row_count + array * tall
            above = pl.multiple_of(base - OFF_Y, SUB)
            out[start : start + tall, :] = first[2 * freqs + array, pl.ds(above, tall), :]


def image_kernel(freqs, offsets, mine, other, image):
    row_count, width = image.shape[2:]
    tall = row_count + 2 * OFF_Y
    lanes = lax.broadcasted_iota(jnp.int32, (row_count, width), 1)
    for h in range(image.shape[1]):
        dy = offsets[0, h]
        dx = offsets[1, h]
        valid = (lanes + dx >= 0) & (lanes + dx < width)
        total = None
        for pack in (mine, other):
            for array in range(2 * freqs):
                source = pack[array * row_count : (array + 1) * row_count, :]
                start = 2 * freqs * row_count + array * tall + OFF_Y
                value = pack[pl.ds(start + dy, row_count), :]
                term = source * pltpu.roll(value, lax.rem(width - dx, width), 1)
                if array >= freqs:
                    term = -term
                total = term if total is None else total + term
        image[0, h] = jnp.where(valid, total, 0.0)


def shards(surface_fields, stencil_table, velocity_bins, offset_list):
    depth_count = lax.axis_size("depth")
    line_count = lax.axis_size("xline")
    row_count = surface_fields.shape[3]
    width = surface_fields.shape[4]
    freqs = surface_fields.shape[2] // 2
    levels = velocity_bins.shape[1]
    grid_rows = row_count * line_count
    row_chunk = next(rows for rows in (64, 32, 16, 8) if grid_rows % rows == 0)

    surf = surface_fields.reshape(1, 4, 2 * freqs, row_count, width)
    bins = velocity_bins
    line_bits = bits_of(line_count)[:-1]
    for bit in line_bits:
        surf = jnp.concatenate([surf, swap(surf, "xline", bit)], axis=0)
    for bit in bits_of(depth_count):
        bins = jnp.concatenate([bins, swap(bins, "depth", bit)], axis=0)
    bins = bins[None]
    for bit in line_bits:
        bins = jnp.concatenate([bins, swap(bins, "xline", bit)], axis=0)
    surf_other = swap(surf, "xline", 1)
    bins_other = swap(bins, "xline", 1)

    sizes = (depth_count, line_count, levels, row_count, freqs, row_chunk)
    field_shape = (4 * freqs, grid_rows + 2 * PAD, width)
    pack_rows = 2 * freqs * (2 * row_count + 2 * OFF_Y)
    pack = jax.ShapeDtypeStruct((pack_rows, width), jnp.float32)
    whole = pl.BlockSpec(memory_space=pltpu.VMEM)
    cells = 2 * (surf.size + bins.size) + 2 * 4 * freqs * field_shape[1] * width
    mine, theirs = pl.pallas_call(
        functools.partial(continuation_kernel, sizes),
        out_shape=[pack, pack],
        in_specs=[whole] * 5,
        out_specs=[whole] * 2,
        scratch_shapes=[
            pltpu.VMEM((len(TAP_ROWS) * 2 * freqs, SUB, width), jnp.float32),
            pltpu.VMEM(field_shape, jnp.float32),
            pltpu.VMEM(field_shape, jnp.float32),
        ],
        compiler_params=pltpu.CompilerParams(vmem_limit_bytes=4 * cells + (2 << 20)),
        name="continuation",
    )(stencil_table, surf, surf_other, bins, bins_other)
    other = swap(theirs, "xline", 1)
    return pl.pallas_call(
        functools.partial(image_kernel, freqs),
        out_shape=jax.ShapeDtypeStruct((1, offset_list.shape[0], row_count, width), jnp.float32),
        in_specs=[pl.BlockSpec(memory_space=pltpu.SMEM), whole, whole],
        out_specs=whole,
        compiler_params=pltpu.CompilerParams(vmem_limit_bytes=4 << 20),
        name="imaging",
    )(offset_list.T, mine, other)


def solution(mesh):
    return jax.shard_map(
        shards,
        mesh=mesh,
        in_specs=(P(None, None, None, "xline", None), P(), P("depth", None, "xline", None), P()),
        out_specs=P("depth", None, "xline", None),
        check_vma=False,
    )
```

```python
import functools

import jax
import jax.numpy as jnp
from jax import lax
from jax.experimental import pallas as pl
from jax.experimental.pallas import tpu as pltpu
from jax.sharding import PartitionSpec as P

OFF_Y = 8
TAP_ROWS = (0, -4, -3, -2, -1, 1, 2, 3, 4, 0, 0, 0, 0)
TAP_COLS = (0, 0, 0, 0, 0, 0, 0, 0, 0, -2, -1, 1, 2)
PAD = 8
SUB = 8
VMEM = pl.BlockSpec(memory_space=pltpu.VMEM)


def bits_of(count):
    return [1 << k for k in reversed(range(count.bit_length() - 1))]


def reversed_bits(value, count):
    width = count.bit_length() - 1
    total = 0
    for k in range(width):
        total = total + (((value >> k) & 1) << (width - 1 - k))
    return total


def odd_bits(value, count):
    width = count.bit_length() - 1
    total = 0
    for k in range(width):
        total = total ^ ((value >> k) & 1)
    return total


def hop(block, depth_bit, line_bit):
    depths, lines = lax.axis_size("depth"), lax.axis_size("xline")
    route = [
        (d * lines + x, (d ^ depth_bit) * lines + (x ^ line_bit))
        for d in range(depths)
        for x in range(lines)
    ]
    return lax.ppermute(block, ("depth", "xline"), route)


def stage_kernel(freqs, table, bins, surf, offsets, wide, bins_out, surf_out, offsets_out):
    parity = lax.axis_index("xline") & 1
    width = surf.shape[-1]
    bins_out[...] = bins[...]
    offsets_out[...] = offsets[...]
    for kind in range(4):
        block = surf[0, kind]
        surf_out[0, kind] = -block if kind == 3 else block
    for tap in range(len(TAP_ROWS)):
        for part in range(2):
            for freq in range(freqs):
                row = table[tap, part, pl.ds(parity * freqs + freq, 1), :]
                wide[(tap * 2 + part) * freqs + freq] = jnp.broadcast_to(row, (SUB, width))


def clear_edges(buffer):
    count, rows, width = buffer.shape
    zeros = jnp.zeros((PAD, width), jnp.float32)
    for array in range(count):
        buffer[array, 0:PAD, :] = zeros
        buffer[array, rows - PAD : rows, :] = zeros


def run_slabs(sizes, start, stop, wide, bins_own, bins_other, first, second):
    depth_count, line_count, levels, row_count, freqs, row_chunk = sizes
    depth_index = lax.axis_index("depth")
    line_index = lax.axis_index("xline")
    width = wide.shape[2]
    grid_rows = row_count * line_count
    near_count = line_count // 2
    lane = lax.broadcasted_iota(jnp.int32, (SUB, width), 1)
    inside = {
        step: (lane + step >= 0) & (lane + step < width) for step in sorted(set(TAP_COLS) - {0})
    }

    def level(slot, odd, level_index, source, target):
        def chunk_step(chunk, carry):
            for block in range(row_chunk // SUB):
                row = pl.multiple_of(chunk * row_chunk + block * SUB, SUB)
                line = (row // row_count) ^ line_index
                near = reversed_bits(line >> 1, near_count)
                inner = pl.multiple_of(row % row_count, SUB)
                own = bins_own[near, slot, level_index, pl.ds(inner, SUB), :]
                other = bins_other[near, slot, level_index, pl.ds(inner, SUB), :]
                crossed = odd ^ odd_bits(line >> 1, near_count)
                bins = jnp.where((line & 1) == crossed, own, other)
                for freq in range(freqs):
                    sums = [None] * 4
                    centre = None
                    for tap in range(len(TAP_ROWS)):
                        coefs = [
                            jnp.take_along_axis(
                                wide[(tap * 2 + part) * freqs + freq],
                                bins,
                                axis=1,
                                mode="promise_in_bounds",
                            )
                            for part in range(2)
                        ]
                        step = TAP_COLS[tap]
                        if step == 0:
                            fields = [
                                source[kind * freqs + freq, pl.ds(PAD + row + TAP_ROWS[tap], SUB), :]
                                for kind in range(4)
                            ]
                            if tap == 0:
                                centre = fields
                        else:
                            fields = [
                                jnp.where(
                                    inside[step], pltpu.roll(value, (-step) % width, 1), 0.0
                                )
                                for value in centre
                            ]
                        for field in range(2):
                            real, imag = fields[2 * field], fields[2 * field + 1]
                            term_real = coefs[0] * real - coefs[1] * imag
                            term_imag = coefs[0] * imag + coefs[1] * real
                            for part, term in ((0, term_real), (1, term_imag)):
                                place = 2 * field + part
                                sums[place] = term if sums[place] is None else sums[place] + term
                    for kind in range(4):
                        target[kind * freqs + freq, pl.ds(PAD + row, SUB), :] = sums[kind]
            return carry

        lax.fori_loop(0, grid_rows // row_chunk, chunk_step, 0)

    def slab_step(slab, carry):
        apart = slab ^ depth_index
        slot = reversed_bits(apart & (depth_count // 2 - 1), depth_count // 2)
        odd = odd_bits(apart, depth_count)
        buffers = (first, second)
        for level_index in range(levels):
            level(slot, odd, level_index, buffers[level_index % 2], buffers[1 - level_index % 2])
        if levels % 2:
            first[...] = second[...]
        return carry

    lax.fori_loop(start, stop, slab_step, 0)


def upper_kernel(sizes, wide, surf_own, surf_other, bins_own, bins_other, state, second):
    depth_count, line_count, _, row_count, freqs, _ = sizes
    depth_index = lax.axis_index("depth")
    line_index = lax.axis_index("xline")
    near_count = line_count // 2
    clear_edges(state)
    clear_edges(second)
    for near in range(near_count):
        odd = near.bit_count() & 1
        for own, source in ((odd, surf_own), (1 - odd, surf_other)):
            line = line_index ^ (2 * reversed_bits(near, near_count) + own)
            start = pl.multiple_of(PAD + line * row_count, SUB)
            for kind in range(4):
                for freq in range(freqs):
                    block = source[near, kind, (line_index & 1) * freqs + freq]
                    state[kind * freqs + freq, pl.ds(start, row_count), :] = block
    half = depth_count // 2
    stop = jnp.where(depth_index >= half, half, 0)
    run_slabs(sizes, 0, stop, wide, bins_own, bins_other, state, second)


def lower_kernel(sizes, wide, bins_own, bins_other, state, mine, theirs, first, second):
    depth_count, _, _, row_count, freqs, _ = sizes
    depth_index = lax.axis_index("depth")
    line_index = lax.axis_index("xline")
    first[...] = state[...]
    clear_edges(second)
    half = depth_count // 2
    start = jnp.where(depth_index >= half, half, 0)
    run_slabs(sizes, start, depth_index + 1, wide, bins_own, bins_other, first, second)
    tall = row_count + 2 * OFF_Y
    for out, line in ((mine, line_index), (theirs, line_index ^ 1)):
        base = pl.multiple_of(PAD + line * row_count, SUB)
        for array in range(2 * freqs):
            out[array * row_count : (array + 1) * row_count, :] = first[
                array, pl.ds(base, row_count), :
            ]
            below = 2 * freqs * row_count + array * tall
            above = pl.multiple_of(base - OFF_Y, SUB)
            out[below : below + tall, :] = first[2 * freqs + array, pl.ds(above, tall), :]


def image_kernel(freqs, offsets, mine, other, image):
    row_count, width = image.shape[2:]
    tall = row_count + 2 * OFF_Y
    lanes = lax.broadcasted_iota(jnp.int32, (row_count, width), 1)
    for h in range(image.shape[1]):
        dy = offsets[0, h]
        dx = offsets[1, h]
        valid = (lanes + dx >= 0) & (lanes + dx < width)
        total = None
        for pack in (mine, other):
            for array in range(2 * freqs):
                source = pack[array * row_count : (array + 1) * row_count, :]
                start = 2 * freqs * row_count + array * tall + OFF_Y
                value = pack[pl.ds(start + dy, row_count), :]
                term = source * pltpu.roll(value, lax.rem(width - dx, width), 1)
                if array >= freqs:
                    term = -term
                total = term if total is None else total + term
        image[0, h] = jnp.where(valid, total, 0.0)


def shards(surface_fields, stencil_table, velocity_bins, offset_list):
    depth_count = lax.axis_size("depth")
    line_count = lax.axis_size("xline")
    row_count = surface_fields.shape[3]
    width = surface_fields.shape[4]
    freqs = surface_fields.shape[2] // 2
    levels = velocity_bins.shape[1]
    grid_rows = row_count * line_count
    row_chunk = next(rows for rows in (64, 32, 16, 8) if grid_rows % rows == 0)
    sizes = (depth_count, line_count, levels, row_count, freqs, row_chunk)
    depth_bits = bits_of(depth_count)
    line_bits = bits_of(line_count)[:-1]
    f32 = jnp.float32

    def call(kernel, outs, scratch, flops, *args):
        size = sum(array.size for array in (*args, *outs)) + sum(ref.shape[0] * ref.shape[1] * ref.shape[2] for ref in scratch)
        return pl.pallas_call(
            kernel,
            out_shape=outs,
            in_specs=[VMEM] * len(args),
            out_specs=[VMEM] * len(outs),
            scratch_shapes=scratch,
            compiler_params=pltpu.CompilerParams(vmem_limit_bytes=4 * size + (2 << 20)),
            cost_estimate=pl.CostEstimate(flops=flops, bytes_accessed=4 * size, transcendentals=0),
        )(*args)

    surf = surface_fields.reshape(1, 4, 2 * freqs, row_count, width)
    offsets = offset_list.T
    like = jax.ShapeDtypeStruct
    wide, bins, surf, offsets = call(
        functools.partial(stage_kernel, freqs),
        [
            like((len(TAP_ROWS) * 2 * freqs, SUB, width), f32),
            like(velocity_bins.shape, velocity_bins.dtype),
            like(surf.shape, f32),
            like(offsets.shape, offsets.dtype),
        ],
        [],
        1000,
        stencil_table,
        velocity_bins,
        surf,
        offsets,
    )

    far = hop(velocity_bins, depth_bits[0], 1)
    near = bins
    for bit in line_bits:
        surf = jnp.concatenate([surf, hop(surf, 0, bit | 1)], axis=0)
    for bit in depth_bits[1:-1]:
        both = hop(jnp.concatenate([far, near], axis=0), bit, 1)
        count = far.shape[0]
        far = jnp.concatenate([far, both[:count]], axis=0)
        near = jnp.concatenate([near, both[count:]], axis=0)
    surf_other = hop(surf, 0, 1)
    far = jnp.concatenate([far, hop(far, depth_bits[-1], 1)], axis=0)[None]
    near = jnp.concatenate([near, hop(near, depth_bits[-1], 1)], axis=0)[None]
    for bit in line_bits:
        far = jnp.concatenate([far, hop(far, 0, bit | 1)], axis=0)
        near = jnp.concatenate([near, hop(near, 0, bit | 1)], axis=0)
    far_other = hop(far, 0, 1)
    near_other = hop(near, 0, 1)

    field_shape = (4 * freqs, grid_rows + 2 * PAD, width)
    field = pltpu.VMEM(field_shape, f32)
    work = depth_count * levels * len(TAP_ROWS) * 8 * field_shape[0] * grid_rows * width
    (state,) = call(
        functools.partial(upper_kernel, sizes),
        [like(field_shape, f32)],
        [field],
        work // 2,
        wide,
        surf,
        surf_other,
        far,
        far_other,
    )
    pack = like((2 * freqs * (2 * row_count + 2 * OFF_Y), width), f32)
    mine, theirs = call(
        functools.partial(lower_kernel, sizes),
        [pack, pack],
        [field, field],
        work // 2,
        wide,
        near,
        near_other,
        state,
    )
    other = hop(theirs, 0, 1)
    image = pl.pallas_call(
        functools.partial(image_kernel, freqs),
        out_shape=like((1, offset_list.shape[0], row_count, width), f32),
        in_specs=[pl.BlockSpec(memory_space=pltpu.SMEM), VMEM, VMEM],
        out_specs=VMEM,
        compiler_params=pltpu.CompilerParams(vmem_limit_bytes=4 << 20),
        name="imaging",
    )(offsets, mine, other)
    return image


def solution(mesh):
    return jax.shard_map(
        shards,
        mesh=mesh,
        in_specs=(P(None, None, None, "xline", None), P(), P("depth", None, "xline", None), P()),
        out_specs=P("depth", None, "xline", None),
        check_vma=False,
    )
```

```python
import functools

import jax
import jax.numpy as jnp
from jax import lax
from jax.experimental import pallas as pl
from jax.experimental.pallas import tpu as pltpu
from jax.sharding import PartitionSpec as P

OFF_Y = 8
TAP_ROWS = (0, -4, -3, -2, -1, 1, 2, 3, 4, 0, 0, 0, 0)
TAP_COLS = (0, 0, 0, 0, 0, 0, 0, 0, 0, -2, -1, 1, 2)
PAD = 8
SUB = 8
VMEM = pl.BlockSpec(memory_space=pltpu.VMEM)


def bits_of(count):
    return [1 << k for k in reversed(range(count.bit_length() - 1))]


def reversed_bits(value, count):
    width = count.bit_length() - 1
    total = 0
    for k in range(width):
        total = total + (((value >> k) & 1) << (width - 1 - k))
    return total


def odd_bits(value, count):
    width = count.bit_length() - 1
    total = 0
    for k in range(width):
        total = total ^ ((value >> k) & 1)
    return total


def hop(block, depth_bit, line_bit):
    depths, lines = lax.axis_size("depth"), lax.axis_size("xline")
    route = [
        (d * lines + x, (d ^ depth_bit) * lines + (x ^ line_bit))
        for d in range(depths)
        for x in range(lines)
    ]
    return lax.ppermute(block, ("depth", "xline"), route)


def load_kernel(bins, bins_out):
    bins_out[...] = bins[...]


def clear_edges(buffer):
    count, rows, width = buffer.shape
    zeros = jnp.zeros((PAD, width), jnp.float32)
    for array in range(count):
        buffer[array, 0:PAD, :] = zeros
        buffer[array, rows - PAD : rows, :] = zeros


def run_slabs(sizes, start, stop, wide, bins_own, bins_other, first, second):
    depth_count, line_count, levels, row_count, freqs, row_chunk = sizes
    depth_index = lax.axis_index("depth")
    line_index = lax.axis_index("xline")
    width = wide.shape[2]
    grid_rows = row_count * line_count
    near_count = line_count // 2
    lane = lax.broadcasted_iota(jnp.int32, (SUB, width), 1)
    inside = {
        step: (lane + step >= 0) & (lane + step < width) for step in sorted(set(TAP_COLS) - {0})
    }

    def level(slot, odd, level_index, source, target):
        def chunk_step(chunk, carry):
            for block in range(row_chunk // SUB):
                row = pl.multiple_of(chunk * row_chunk + block * SUB, SUB)
                line = (row // row_count) ^ line_index
                near = reversed_bits(line >> 1, near_count)
                inner = pl.multiple_of(row % row_count, SUB)
                own = bins_own[near, slot, level_index, pl.ds(inner, SUB), :]
                other = bins_other[near, slot, level_index, pl.ds(inner, SUB), :]
                crossed = odd ^ odd_bits(line >> 1, near_count)
                bins = jnp.where((line & 1) == crossed, own, other)
                for freq in range(freqs):
                    sums = [None] * 4
                    centre = None
                    for tap in range(len(TAP_ROWS)):
                        coefs = [
                            jnp.take_along_axis(
                                wide[(tap * 2 + part) * freqs + freq],
                                bins,
                                axis=1,
                                mode="promise_in_bounds",
                            )
                            for part in range(2)
                        ]
                        step = TAP_COLS[tap]
                        if step == 0:
                            fields = [
                                source[kind * freqs + freq, pl.ds(PAD + row + TAP_ROWS[tap], SUB), :]
                                for kind in range(4)
                            ]
                            if tap == 0:
                                centre = fields
                        else:
                            fields = [
                                jnp.where(
                                    inside[step], pltpu.roll(value, (-step) % width, 1), 0.0
                                )
                                for value in centre
                            ]
                        for field in range(2):
                            real, imag = fields[2 * field], fields[2 * field + 1]
                            term_real = coefs[0] * real - coefs[1] * imag
                            term_imag = coefs[0] * imag + coefs[1] * real
                            for part, term in ((0, term_real), (1, term_imag)):
                                place = 2 * field + part
                                sums[place] = term if sums[place] is None else sums[place] + term
                    for kind in range(4):
                        target[kind * freqs + freq, pl.ds(PAD + row, SUB), :] = sums[kind]
            return carry

        lax.fori_loop(0, grid_rows // row_chunk, chunk_step, 0)

    def slab_step(slab, carry):
        apart = slab ^ depth_index
        slot = reversed_bits(apart & (depth_count // 2 - 1), depth_count // 2)
        odd = odd_bits(apart, depth_count)
        buffers = (first, second)
        for level_index in range(levels):
            level(slot, odd, level_index, buffers[level_index % 2], buffers[1 - level_index % 2])
        if levels % 2:
            first[...] = second[...]
        return carry

    lax.fori_loop(start, stop, slab_step, 0)


def upper_kernel(
    sizes,
    table,
    offsets,
    surf_own,
    surf_other,
    bins_own,
    bins_other,
    wide,
    offsets_out,
    state,
    second,
):
    depth_count, line_count, _, row_count, freqs, _ = sizes
    depth_index = lax.axis_index("depth")
    line_index = lax.axis_index("xline")
    near_count = line_count // 2
    parity = line_index & 1
    offsets_out[...] = offsets[...]
    for tap in range(len(TAP_ROWS)):
        for part in range(2):
            for freq in range(freqs):
                row = table[tap, part, pl.ds(parity * freqs + freq, 1), :]
                wide[(tap * 2 + part) * freqs + freq] = jnp.broadcast_to(row, wide.shape[1:])
    clear_edges(state)
    clear_edges(second)
    for near in range(near_count):
        odd = near.bit_count() & 1
        for own, source in ((odd, surf_own), (1 - odd, surf_other)):
            line = line_index ^ (2 * reversed_bits(near, near_count) + own)
            start = pl.multiple_of(PAD + line * row_count, SUB)
            for kind in range(4):
                for freq in range(freqs):
                    block = source[near, kind, parity * freqs + freq]
                    if kind == 3:
                        block = -block
                    state[kind * freqs + freq, pl.ds(start, row_count), :] = block
    half = depth_count // 2
    stop = jnp.where(depth_index >= half, half, 0)
    run_slabs(sizes, 0, stop, wide, bins_own, bins_other, state, second)


def lower_kernel(sizes, wide, bins_own, bins_other, state, mine, theirs, first, second):
    depth_count, _, _, row_count, freqs, _ = sizes
    depth_index = lax.axis_index("depth")
    line_index = lax.axis_index("xline")
    first[...] = state[...]
    clear_edges(second)
    half = depth_count // 2
    start = jnp.where(depth_index >= half, half, 0)
    run_slabs(sizes, start, depth_index + 1, wide, bins_own, bins_other, first, second)
    tall = row_count + 2 * OFF_Y
    for out, line in ((mine, line_index), (theirs, line_index ^ 1)):
        base = pl.multiple_of(PAD + line * row_count, SUB)
        for array in range(2 * freqs):
            out[array * row_count : (array + 1) * row_count, :] = first[
                array, pl.ds(base, row_count), :
            ]
            below = 2 * freqs * row_count + array * tall
            above = pl.multiple_of(base - OFF_Y, SUB)
            out[below : below + tall, :] = first[2 * freqs + array, pl.ds(above, tall), :]


def image_kernel(freqs, offsets, mine, other, image):
    row_count, width = image.shape[2:]
    tall = row_count + 2 * OFF_Y
    lanes = lax.broadcasted_iota(jnp.int32, (row_count, width), 1)
    for h in range(image.shape[1]):
        dy = offsets[0, h]
        dx = offsets[1, h]
        valid = (lanes + dx >= 0) & (lanes + dx < width)
        total = None
        for pack in (mine, other):
            for array in range(2 * freqs):
                source = pack[array * row_count : (array + 1) * row_count, :]
                start = 2 * freqs * row_count + array * tall + OFF_Y
                value = pack[pl.ds(start + dy, row_count), :]
                term = source * pltpu.roll(value, lax.rem(width - dx, width), 1)
                if array >= freqs:
                    term = -term
                total = term if total is None else total + term
        image[0, h] = jnp.where(valid, total, 0.0)


def shards(surface_fields, stencil_table, velocity_bins, offset_list):
    depth_count = lax.axis_size("depth")
    line_count = lax.axis_size("xline")
    row_count = surface_fields.shape[3]
    width = surface_fields.shape[4]
    freqs = surface_fields.shape[2] // 2
    levels = velocity_bins.shape[1]
    grid_rows = row_count * line_count
    row_chunk = next(rows for rows in (64, 32, 16, 8) if grid_rows % rows == 0)
    sizes = (depth_count, line_count, levels, row_count, freqs, row_chunk)
    depth_bits = bits_of(depth_count)
    line_bits = bits_of(line_count)[:-1]
    f32 = jnp.float32

    def call(kernel, outs, scratch, flops, *args):
        size = sum(array.size for array in (*args, *outs, *scratch))
        return pl.pallas_call(
            kernel,
            out_shape=outs,
            in_specs=[VMEM] * len(args),
            out_specs=[VMEM] * len(outs),
            scratch_shapes=[pltpu.VMEM(array.shape, array.dtype) for array in scratch],
            compiler_params=pltpu.CompilerParams(vmem_limit_bytes=4 * size + (2 << 20)),
            cost_estimate=pl.CostEstimate(flops=flops, bytes_accessed=4 * size, transcendentals=0),
        )(*args)

    like = jax.ShapeDtypeStruct
    surf = surface_fields.reshape(1, 4, 2 * freqs, row_count, width)
    (bins,) = call(
        load_kernel, [like(velocity_bins.shape, velocity_bins.dtype)], [], 1000, velocity_bins
    )

    far = hop(velocity_bins, depth_bits[0], 1)
    near = bins
    for bit in line_bits:
        surf = jnp.concatenate([surf, hop(surf, 0, bit | 1)], axis=0)
    for bit in depth_bits[1:-1]:
        both = hop(jnp.concatenate([far, near], axis=0), bit, 1)
        count = far.shape[0]
        far = jnp.concatenate([far, both[:count]], axis=0)
        near = jnp.concatenate([near, both[count:]], axis=0)
    surf_other = hop(surf, 0, 1)
    far = jnp.concatenate([far, hop(far, depth_bits[-1], 1)], axis=0)[None]
    near = jnp.concatenate([near, hop(near, depth_bits[-1], 1)], axis=0)[None]
    for bit in line_bits:
        far = jnp.concatenate([far, hop(far, 0, bit | 1)], axis=0)
        near = jnp.concatenate([near, hop(near, 0, bit | 1)], axis=0)
    far_other = hop(far, 0, 1)
    near_other = hop(near, 0, 1)

    field_shape = (4 * freqs, grid_rows + 2 * PAD, width)
    field = like(field_shape, f32)
    work = depth_count * levels * len(TAP_ROWS) * 8 * field_shape[0] * grid_rows * width
    offsets = offset_list.T
    wide, offsets, state = call(
        functools.partial(upper_kernel, sizes),
        [
            like((len(TAP_ROWS) * 2 * freqs, SUB, width), f32),
            like(offsets.shape, offsets.dtype),
            field,
        ],
        [field],
        work // 2,
        stencil_table,
        offsets,
        surf,
        surf_other,
        far,
        far_other,
    )
    pack = like((2 * freqs * (2 * row_count + 2 * OFF_Y), width), f32)
    mine, theirs = call(
        functools.partial(lower_kernel, sizes),
        [pack, pack],
        [field, field],
        work // 2,
        wide,
        near,
        near_other,
        state,
    )
    other = hop(theirs, 0, 1)
    image = pl.pallas_call(
        functools.partial(image_kernel, freqs),
        out_shape=like((1, offset_list.shape[0], row_count, width), f32),
        in_specs=[pl.BlockSpec(memory_space=pltpu.SMEM), VMEM, VMEM],
        out_specs=VMEM,
        compiler_params=pltpu.CompilerParams(vmem_limit_bytes=4 << 20),
        name="imaging",
    )(offsets, mine, other)
    return image


def solution(mesh):
    return jax.shard_map(
        shards,
        mesh=mesh,
        in_specs=(P(None, None, None, "xline", None), P(), P("depth", None, "xline", None), P()),
        out_specs=P("depth", None, "xline", None),
        check_vma=False,
    )
```

```python
import functools

import jax
import jax.numpy as jnp
from jax import lax
from jax.experimental import pallas as pl
from jax.experimental.pallas import tpu as pltpu
from jax.sharding import PartitionSpec as P

OFF_Y = 8
TAP_ROWS = (0, -4, -3, -2, -1, 1, 2, 3, 4, 0, 0, 0, 0)
TAP_COLS = (0, 0, 0, 0, 0, 0, 0, 0, 0, -2, -1, 1, 2)
PAD = 8
SUB = 8
VMEM = pl.BlockSpec(memory_space=pltpu.VMEM)


def bits_of(count):
    return [1 << k for k in reversed(range(count.bit_length() - 1))]


def reversed_bits(value, count):
    width = count.bit_length() - 1
    total = 0
    for k in range(width):
        total = total + (((value >> k) & 1) << (width - 1 - k))
    return total


def odd_bits(value, count):
    width = count.bit_length() - 1
    total = 0
    for k in range(width):
        total = total ^ ((value >> k) & 1)
    return total


def hop(block, depth_bit, line_bit):
    depths, lines = lax.axis_size("depth"), lax.axis_size("xline")
    route = [
        (d * lines + x, (d ^ depth_bit) * lines + (x ^ line_bit))
        for d in range(depths)
        for x in range(lines)
    ]
    return lax.ppermute(block, ("depth", "xline"), route)


def load_kernel(bins, bins_out):
    bins_out[...] = bins[...]


def clear_edges(buffer):
    count, rows, width = buffer.shape
    zeros = jnp.zeros((PAD, width), jnp.float32)
    for array in range(count):
        buffer[array, 0:PAD, :] = zeros
        buffer[array, rows - PAD : rows, :] = zeros


def run_slabs(sizes, start, stop, wide, bins_own, bins_other, first, second):
    depth_count, line_count, levels, row_count, freqs, row_chunk = sizes
    depth_index = lax.axis_index("depth")
    line_index = lax.axis_index("xline")
    width = wide.shape[2]
    grid_rows = row_count * line_count
    near_count = line_count // 2
    lane = lax.broadcasted_iota(jnp.int32, (SUB, width), 1)
    inside = {
        step: (lane + step >= 0) & (lane + step < width) for step in sorted(set(TAP_COLS) - {0})
    }

    def level(slot, odd, level_index, source, target):
        def chunk_step(chunk, carry):
            for block in range(row_chunk // SUB):
                row = pl.multiple_of(chunk * row_chunk + block * SUB, SUB)
                line = (row // row_count) ^ line_index
                near = reversed_bits(line >> 1, near_count)
                inner = pl.multiple_of(row % row_count, SUB)
                own = bins_own[near, slot, level_index, pl.ds(inner, SUB), :]
                other = bins_other[near, slot, level_index, pl.ds(inner, SUB), :]
                crossed = odd ^ odd_bits(line >> 1, near_count)
                bins = jnp.where((line & 1) == crossed, own, other)
                for freq in range(freqs):
                    sums = [None] * 4
                    centre = None
                    for tap in range(len(TAP_ROWS)):
                        coefs = [
                            jnp.take_along_axis(
                                wide[(tap * 2 + part) * freqs + freq],
                                bins,
                                axis=1,
                                mode="promise_in_bounds",
                            )
                            for part in range(2)
                        ]
                        step = TAP_COLS[tap]
                        if step == 0:
                            fields = [
                                source[kind * freqs + freq, pl.ds(PAD + row + TAP_ROWS[tap], SUB), :]
                                for kind in range(4)
                            ]
                            if tap == 0:
                                centre = fields
                        else:
                            fields = [
                                jnp.where(
                                    inside[step], pltpu.roll(value, (-step) % width, 1), 0.0
                                )
                                for value in centre
                            ]
                        for field in range(2):
                            real, imag = fields[2 * field], fields[2 * field + 1]
                            term_real = coefs[0] * real - coefs[1] * imag
                            term_imag = coefs[0] * imag + coefs[1] * real
                            for part, term in ((0, term_real), (1, term_imag)):
                                place = 2 * field + part
                                sums[place] = term if sums[place] is None else sums[place] + term
                    for kind in range(4):
                        target[kind * freqs + freq, pl.ds(PAD + row, SUB), :] = sums[kind]
            return carry

        lax.fori_loop(0, grid_rows // row_chunk, chunk_step, 0)

    def slab_step(slab, carry):
        apart = slab ^ depth_index
        slot = reversed_bits(apart & (depth_count // 2 - 1), depth_count // 2)
        odd = odd_bits(apart, depth_count)
        buffers = (first, second)
        for level_index in range(levels):
            level(slot, odd, level_index, buffers[level_index % 2], buffers[1 - level_index % 2])
        if levels % 2:
            first[...] = second[...]
        return carry

    lax.fori_loop(start, stop, slab_step, 0)


def far_slabs(depth_count, first_part):
    half = depth_count // 2
    count = jnp.where(lax.axis_index("depth") >= half, half, 0)
    return (0, count // 2) if first_part else (count // 2, count)


def begin_kernel(
    sizes,
    table,
    offsets,
    surf_own,
    surf_other,
    bins_own,
    bins_other,
    wide,
    offsets_out,
    state,
    second,
):
    depth_count, line_count, _, row_count, freqs, _ = sizes
    line_index = lax.axis_index("xline")
    near_count = line_count // 2
    parity = line_index & 1
    offsets_out[...] = offsets[...]
    for tap in range(len(TAP_ROWS)):
        for part in range(2):
            for freq in range(freqs):
                row = table[tap, part, pl.ds(parity * freqs + freq, 1), :]
                wide[(tap * 2 + part) * freqs + freq] = jnp.broadcast_to(row, wide.shape[1:])
    clear_edges(state)
    clear_edges(second)
    for near in range(near_count):
        odd = near.bit_count() & 1
        for own, source in ((odd, surf_own), (1 - odd, surf_other)):
            line = line_index ^ (2 * reversed_bits(near, near_count) + own)
            start = pl.multiple_of(PAD + line * row_count, SUB)
            for kind in range(4):
                for freq in range(freqs):
                    block = source[near, kind, parity * freqs + freq]
                    if kind == 3:
                        block = -block
                    state[kind * freqs + freq, pl.ds(start, row_count), :] = block
    run_slabs(sizes, *far_slabs(depth_count, True), wide, bins_own, bins_other, state, second)


def middle_kernel(sizes, wide, bins_own, bins_other, before, state, second):
    state[...] = before[...]
    clear_edges(second)
    run_slabs(sizes, *far_slabs(sizes[0], False), wide, bins_own, bins_other, state, second)


def finish_kernel(sizes, wide, bins_own, bins_other, before, mine, theirs, first, second):
    depth_count, _, _, row_count, freqs, _ = sizes
    depth_index = lax.axis_index("depth")
    line_index = lax.axis_index("xline")
    first[...] = before[...]
    clear_edges(second)
    start = jnp.where(depth_index >= depth_count // 2, depth_count // 2, 0)
    run_slabs(sizes, start, depth_index + 1, wide, bins_own, bins_other, first, second)
    tall = row_count + 2 * OFF_Y
    for out, line in ((mine, line_index), (theirs, line_index ^ 1)):
        base = pl.multiple_of(PAD + line * row_count, SUB)
        for array in range(2 * freqs):
            out[array * row_count : (array + 1) * row_count, :] = first[
                array, pl.ds(base, row_count), :
            ]
            below = 2 * freqs * row_count + array * tall
            above = pl.multiple_of(base - OFF_Y, SUB)
            out[below : below + tall, :] = first[2 * freqs + array, pl.ds(above, tall), :]


def image_kernel(freqs, offsets, mine, other, image):
    row_count, width = image.shape[2:]
    tall = row_count + 2 * OFF_Y
    lanes = lax.broadcasted_iota(jnp.int32, (row_count, width), 1)
    for h in range(image.shape[1]):
        dy = offsets[0, h]
        dx = offsets[1, h]
        valid = (lanes + dx >= 0) & (lanes + dx < width)
        total = None
        for pack in (mine, other):
            for array in range(2 * freqs):
                source = pack[array * row_count : (array + 1) * row_count, :]
                start = 2 * freqs * row_count + array * tall + OFF_Y
                value = pack[pl.ds(start + dy, row_count), :]
                term = source * pltpu.roll(value, lax.rem(width - dx, width), 1)
                if array >= freqs:
                    term = -term
                total = term if total is None else total + term
        image[0, h] = jnp.where(valid, total, 0.0)


def shards(surface_fields, stencil_table, velocity_bins, offset_list):
    depth_count = lax.axis_size("depth")
    line_count = lax.axis_size("xline")
    row_count = surface_fields.shape[3]
    width = surface_fields.shape[4]
    freqs = surface_fields.shape[2] // 2
    levels = velocity_bins.shape[1]
    grid_rows = row_count * line_count
    row_chunk = next(rows for rows in (64, 32, 16, 8) if grid_rows % rows == 0)
    sizes = (depth_count, line_count, levels, row_count, freqs, row_chunk)
    depth_bits = bits_of(depth_count)
    line_bits = bits_of(line_count)[:-1]
    f32 = jnp.float32

    def call(kernel, outs, scratch, flops, *args):
        size = sum(array.size for array in (*args, *outs, *scratch))
        return pl.pallas_call(
            kernel,
            out_shape=outs,
            in_specs=[VMEM] * len(args),
            out_specs=[VMEM] * len(outs),
            scratch_shapes=[pltpu.VMEM(array.shape, array.dtype) for array in scratch],
            compiler_params=pltpu.CompilerParams(vmem_limit_bytes=4 * size + (2 << 20)),
            cost_estimate=pl.CostEstimate(flops=flops, bytes_accessed=4 * size, transcendentals=0),
        )(*args)

    like = jax.ShapeDtypeStruct
    surf = surface_fields.reshape(1, 4, 2 * freqs, row_count, width)
    (bins,) = call(
        load_kernel, [like(velocity_bins.shape, velocity_bins.dtype)], [], 1000, velocity_bins
    )

    top, below = depth_bits[:2]
    last, line = depth_bits[-1], line_bits[0]
    from_top, from_both, from_below = [
        hop(velocity_bins, bit, bit.bit_count() & 1)
        for bit in (top, top | below, below)
    ]
    far = jnp.concatenate([from_top, from_both], axis=0)
    near = jnp.concatenate([bins, from_below], axis=0)
    surf = jnp.concatenate([surf, hop(surf, 0, line | 1)], axis=0)
    for bit in depth_bits[2:-1]:
        part = hop(jnp.concatenate([far, near], axis=0), bit, 1)
        far = jnp.concatenate([far, part[: far.shape[0]]], axis=0)
        near = jnp.concatenate([near, part[near.shape[0] :]], axis=0)
    part = hop(jnp.concatenate([far, near], axis=0), last, 1)
    count = far.shape[0]

    def along_line(bins, deeper):
        line_part = hop(bins, 0, line | 1)
        cross_part = hop(bins, last, line)
        bins = jnp.stack(
            [
                jnp.concatenate([bins, deeper], axis=0),
                jnp.concatenate([line_part, cross_part], axis=0),
            ]
        )
        for bit in line_bits[1:]:
            bins = jnp.concatenate([bins, hop(bins, 0, bit | 1)], axis=0)
        return bins, hop(bins, 0, 1)

    far, far_other = along_line(far, part[:count])
    near, near_other = along_line(near, part[count:])
    for bit in line_bits[1:]:
        surf = jnp.concatenate([surf, hop(surf, 0, bit | 1)], axis=0)
    surf_other = hop(surf, 0, 1)

    field_shape = (4 * freqs, grid_rows + 2 * PAD, width)
    field = like(field_shape, f32)
    work = depth_count * levels * len(TAP_ROWS) * 8 * field_shape[0] * grid_rows * width
    offsets = offset_list.T
    wide, offsets, state = call(
        functools.partial(begin_kernel, sizes),
        [
            like((len(TAP_ROWS) * 2 * freqs, SUB, width), f32),
            like(offsets.shape, offsets.dtype),
            field,
        ],
        [field],
        work // 4,
        stencil_table,
        offsets,
        surf,
        surf_other,
        far,
        far_other,
    )
    (state,) = call(
        functools.partial(middle_kernel, sizes),
        [field],
        [field],
        work // 4,
        wide,
        far,
        far_other,
        state,
    )
    pack = like((2 * freqs * (2 * row_count + 2 * OFF_Y), width), f32)
    mine, theirs = call(
        functools.partial(finish_kernel, sizes),
        [pack, pack],
        [field, field],
        work // 2,
        wide,
        near,
        near_other,
        state,
    )
    other = hop(theirs, 0, 1)
    image = pl.pallas_call(
        functools.partial(image_kernel, freqs),
        out_shape=like((1, offset_list.shape[0], row_count, width), f32),
        in_specs=[pl.BlockSpec(memory_space=pltpu.SMEM), VMEM, VMEM],
        out_specs=VMEM,
        compiler_params=pltpu.CompilerParams(vmem_limit_bytes=4 << 20),
        name="imaging",
    )(offsets, mine, other)
    return image


def solution(mesh):
    return jax.shard_map(
        shards,
        mesh=mesh,
        in_specs=(P(None, None, None, "xline", None), P(), P("depth", None, "xline", None), P()),
        out_specs=P("depth", None, "xline", None),
        check_vma=False,
    )
```

```python
import functools

import jax
import jax.numpy as jnp
from jax import lax
from jax.experimental import pallas as pl
from jax.experimental.pallas import tpu as pltpu
from jax.sharding import PartitionSpec as P

OFF_Y = 8
TAP_ROWS = (0, -4, -3, -2, -1, 1, 2, 3, 4, 0, 0, 0, 0)
TAP_COLS = (0, 0, 0, 0, 0, 0, 0, 0, 0, -2, -1, 1, 2)
PAD = 8
SUB = 8
VMEM = pl.BlockSpec(memory_space=pltpu.VMEM)


def bits_of(count):
    return [1 << k for k in reversed(range(count.bit_length() - 1))]


def reversed_bits(value, count):
    width = count.bit_length() - 1
    total = 0
    for k in range(width):
        total = total + (((value >> k) & 1) << (width - 1 - k))
    return total


def odd_bits(value, count):
    width = count.bit_length() - 1
    total = 0
    for k in range(width):
        total = total ^ ((value >> k) & 1)
    return total


def hop(block, depth_bit, line_bit):
    depths, lines = lax.axis_size("depth"), lax.axis_size("xline")
    route = [
        (d * lines + x, (d ^ depth_bit) * lines + (x ^ line_bit))
        for d in range(depths)
        for x in range(lines)
    ]
    return lax.ppermute(block, ("depth", "xline"), route)


def load_kernel(bins, bins_out):
    bins_out[...] = bins[...]


def clear_edges(buffer):
    count, rows, width = buffer.shape
    zeros = jnp.zeros((PAD, width), jnp.float32)
    for array in range(count):
        buffer[array, 0:PAD, :] = zeros
        buffer[array, rows - PAD : rows, :] = zeros


def run_slabs(sizes, start, stop, wide, bins_own, bins_other, first, second):
    depth_count, line_count, levels, row_count, freqs, row_chunk = sizes
    depth_index = lax.axis_index("depth")
    line_index = lax.axis_index("xline")
    width = wide.shape[2]
    grid_rows = row_count * line_count
    near_count = line_count // 2
    lane = lax.broadcasted_iota(jnp.int32, (SUB, width), 1)
    inside = {
        step: (lane + step >= 0) & (lane + step < width) for step in sorted(set(TAP_COLS) - {0})
    }

    def level(slot, odd, level_index, source, target):
        def chunk_step(chunk, carry):
            for block in range(row_chunk // SUB):
                row = pl.multiple_of(chunk * row_chunk + block * SUB, SUB)
                line = (row // row_count) ^ line_index
                near = reversed_bits(line >> 1, near_count)
                inner = pl.multiple_of(row % row_count, SUB)
                own = bins_own[near, slot, level_index, pl.ds(inner, SUB), :]
                other = bins_other[near, slot, level_index, pl.ds(inner, SUB), :]
                crossed = odd ^ odd_bits(line >> 1, near_count)
                bins = jnp.where((line & 1) == crossed, own, other)
                for freq in range(freqs):
                    sums = [None] * 4
                    centre = None
                    for tap in range(len(TAP_ROWS)):
                        coefs = [
                            jnp.take_along_axis(
                                wide[(tap * 2 + part) * freqs + freq],
                                bins,
                                axis=1,
                                mode="promise_in_bounds",
                            )
                            for part in range(2)
                        ]
                        step = TAP_COLS[tap]
                        if step == 0:
                            fields = [
                                source[kind * freqs + freq, pl.ds(PAD + row + TAP_ROWS[tap], SUB), :]
                                for kind in range(4)
                            ]
                            if tap == 0:
                                centre = fields
                        else:
                            fields = [
                                jnp.where(
                                    inside[step], pltpu.roll(value, (-step) % width, 1), 0.0
                                )
                                for value in centre
                            ]
                        for field in range(2):
                            real, imag = fields[2 * field], fields[2 * field + 1]
                            term_real = coefs[0] * real - coefs[1] * imag
                            term_imag = coefs[0] * imag + coefs[1] * real
                            for part, term in ((0, term_real), (1, term_imag)):
                                place = 2 * field + part
                                sums[place] = term if sums[place] is None else sums[place] + term
                    for kind in range(4):
                        target[kind * freqs + freq, pl.ds(PAD + row, SUB), :] = sums[kind]
            return carry

        lax.fori_loop(0, grid_rows // row_chunk, chunk_step, 0)

    def slab_step(slab, carry):
        apart = slab ^ depth_index
        slot = reversed_bits(apart, depth_count)
        odd = odd_bits(apart, depth_count)
        buffers = (first, second)
        for level_index in range(levels):
            level(slot, odd, level_index, buffers[level_index % 2], buffers[1 - level_index % 2])
        if levels % 2:
            first[...] = second[...]
        return carry

    lax.fori_loop(start, stop, slab_step, 0)


def continuation_kernel(
    sizes,
    table,
    offsets,
    surf_own,
    surf_other,
    bins_own,
    bins_other,
    mine,
    theirs,
    offsets_out,
    wide,
    first,
    second,
):
    _, line_count, _, row_count, freqs, _ = sizes
    depth_index = lax.axis_index("depth")
    line_index = lax.axis_index("xline")
    near_count = line_count // 2
    parity = line_index & 1
    offsets_out[...] = offsets[...]
    for tap in range(len(TAP_ROWS)):
        for part in range(2):
            for freq in range(freqs):
                row = table[tap, part, pl.ds(parity * freqs + freq, 1), :]
                wide[(tap * 2 + part) * freqs + freq] = jnp.broadcast_to(row, wide.shape[1:])
    clear_edges(first)
    clear_edges(second)
    for near in range(near_count):
        odd = near.bit_count() & 1
        for own, source in ((odd, surf_own), (1 - odd, surf_other)):
            line = line_index ^ (2 * reversed_bits(near, near_count) + own)
            start = pl.multiple_of(PAD + line * row_count, SUB)
            for kind in range(4):
                for freq in range(freqs):
                    block = source[near, kind, parity * freqs + freq]
                    if kind == 3:
                        block = -block
                    first[kind * freqs + freq, pl.ds(start, row_count), :] = block
    run_slabs(sizes, 0, depth_index + 1, wide, bins_own, bins_other, first, second)
    tall = row_count + 2 * OFF_Y
    for out, line in ((mine, line_index), (theirs, line_index ^ 1)):
        base = pl.multiple_of(PAD + line * row_count, SUB)
        for array in range(2 * freqs):
            out[array * row_count : (array + 1) * row_count, :] = first[
                array, pl.ds(base, row_count), :
            ]
            below = 2 * freqs * row_count + array * tall
            above = pl.multiple_of(base - OFF_Y, SUB)
            out[below : below + tall, :] = first[2 * freqs + array, pl.ds(above, tall), :]


def image_kernel(freqs, offsets, mine, other, image):
    row_count, width = image.shape[2:]
    tall = row_count + 2 * OFF_Y
    lanes = lax.broadcasted_iota(jnp.int32, (row_count, width), 1)
    for h in range(image.shape[1]):
        dy = offsets[0, h]
        dx = offsets[1, h]
        valid = (lanes + dx >= 0) & (lanes + dx < width)
        total = None
        for pack in (mine, other):
            for array in range(2 * freqs):
                source = pack[array * row_count : (array + 1) * row_count, :]
                start = 2 * freqs * row_count + array * tall + OFF_Y
                value = pack[pl.ds(start + dy, row_count), :]
                term = source * pltpu.roll(value, lax.rem(width - dx, width), 1)
                if array >= freqs:
                    term = -term
                total = term if total is None else total + term
        image[0, h] = jnp.where(valid, total, 0.0)


def shards(surface_fields, stencil_table, velocity_bins, offset_list):
    depth_count = lax.axis_size("depth")
    line_count = lax.axis_size("xline")
    row_count = surface_fields.shape[3]
    width = surface_fields.shape[4]
    freqs = surface_fields.shape[2] // 2
    levels = velocity_bins.shape[1]
    grid_rows = row_count * line_count
    row_chunk = next(rows for rows in (64, 32, 16, 8) if grid_rows % rows == 0)
    sizes = (depth_count, line_count, levels, row_count, freqs, row_chunk)
    depth_bits = bits_of(depth_count)
    line_bits = bits_of(line_count)[:-1]
    f32 = jnp.float32

    def call(kernel, outs, scratch, flops, *args):
        size = sum(array.size for array in (*args, *outs, *scratch))
        return pl.pallas_call(
            kernel,
            out_shape=outs,
            in_specs=[VMEM] * len(args),
            out_specs=[VMEM] * len(outs),
            scratch_shapes=[pltpu.VMEM(array.shape, array.dtype) for array in scratch],
            compiler_params=pltpu.CompilerParams(vmem_limit_bytes=4 * size + (2 << 20)),
            cost_estimate=pl.CostEstimate(flops=flops, bytes_accessed=4 * size, transcendentals=0),
        )(*args)

    like = jax.ShapeDtypeStruct
    surf = surface_fields.reshape(1, 4, 2 * freqs, row_count, width)
    (bins,) = call(
        load_kernel, [like(velocity_bins.shape, velocity_bins.dtype)], [], 1000, velocity_bins
    )

    top, below = depth_bits[:2]
    last, line = depth_bits[-1], line_bits[0]
    parts = [velocity_bins] + [
        hop(velocity_bins, bit, bit.bit_count() & 1)
        for bit in (top, top | below, below)
    ]
    parts[0] = bins
    bins = jnp.concatenate([parts[0], parts[1], parts[3], parts[2]], axis=0)
    surf = jnp.concatenate([surf, hop(surf, 0, line | 1)], axis=0)
    for bit in depth_bits[2:-1]:
        bins = jnp.concatenate([bins, hop(bins, bit, 1)], axis=0)
    depth_part = hop(bins, last, 1)
    line_part = hop(bins, 0, line | 1)
    cross_part = hop(bins, last, line)
    bins = jnp.stack(
        [
            jnp.concatenate([bins, depth_part], axis=0),
            jnp.concatenate([line_part, cross_part], axis=0),
        ]
    )
    for bit in line_bits[1:]:
        bins = jnp.concatenate([bins, hop(bins, 0, bit | 1)], axis=0)
        surf = jnp.concatenate([surf, hop(surf, 0, bit | 1)], axis=0)
    surf_other = hop(surf, 0, 1)
    bins_other = hop(bins, 0, 1)

    field_shape = (4 * freqs, grid_rows + 2 * PAD, width)
    field = like(field_shape, f32)
    work = depth_count * levels * len(TAP_ROWS) * 8 * field_shape[0] * grid_rows * width
    pack = like((2 * freqs * (2 * row_count + 2 * OFF_Y), width), f32)
    offsets = offset_list.T
    mine, theirs, offsets = call(
        functools.partial(continuation_kernel, sizes),
        [pack, pack, like(offsets.shape, offsets.dtype)],
        [like((len(TAP_ROWS) * 2 * freqs, SUB, width), f32), field, field],
        work,
        stencil_table,
        offsets,
        surf,
        surf_other,
        bins,
        bins_other,
    )
    other = hop(theirs, 0, 1)
    image = pl.pallas_call(
        functools.partial(image_kernel, freqs),
        out_shape=like((1, offset_list.shape[0], row_count, width), f32),
        in_specs=[VMEM, VMEM, VMEM],
        out_specs=VMEM,
        compiler_params=pltpu.CompilerParams(vmem_limit_bytes=4 << 20),
        name="imaging",
    )(offsets, mine, other)
    return image


def solution(mesh):
    return jax.shard_map(
        shards,
        mesh=mesh,
        in_specs=(P(None, None, None, "xline", None), P(), P("depth", None, "xline", None), P()),
        out_specs=P("depth", None, "xline", None),
        check_vma=False,
    )
```

```python
import functools

import jax
import jax.numpy as jnp
from jax import lax
from jax.experimental import pallas as pl
from jax.experimental.pallas import tpu as pltpu
from jax.sharding import PartitionSpec as P

OFF_Y = 8
TAP_ROWS = (0, -4, -3, -2, -1, 1, 2, 3, 4, 0, 0, 0, 0)
TAP_COLS = (0, 0, 0, 0, 0, 0, 0, 0, 0, -2, -1, 1, 2)
PAD = 8
SUB = 8
CHUNK = 8
REACH_ROWS = 4
STEPS = (-2, -1, 1, 2)
PARTS = 2
VMEM = pl.BlockSpec(memory_space=pltpu.VMEM)


def bits_of(count):
    return [1 << k for k in reversed(range(count.bit_length() - 1))]


def reversed_bits(value, count):
    width = count.bit_length() - 1
    total = 0
    for k in range(width):
        total = total + (((value >> k) & 1) << (width - 1 - k))
    return total


def odd_bits(value, count):
    width = count.bit_length() - 1
    total = 0
    for k in range(width):
        total = total ^ ((value >> k) & 1)
    return total


def hop(block, depth_bit, line_bit):
    depths, lines = lax.axis_size("depth"), lax.axis_size("xline")
    route = [
        (d * lines + x, (d ^ depth_bit) * lines + (x ^ line_bit))
        for d in range(depths)
        for x in range(lines)
    ]
    return lax.ppermute(block, ("depth", "xline"), route)


def load_kernel(bins, bins_out):
    bins_out[...] = bins[...]


def clear_edges(buffer):
    count, rows, width = buffer.shape
    zeros = jnp.zeros((PAD, width), jnp.float32)
    for array in range(count):
        buffer[array, 0:PAD, :] = zeros
        buffer[array, rows - PAD : rows, :] = zeros


def build_shifts(shifts, width):
    source = lax.broadcasted_iota(jnp.int32, (width, width), 0)
    target = lax.broadcasted_iota(jnp.int32, (width, width), 1)
    for k, step in enumerate(STEPS):
        matrix = (source == target + step).astype(jnp.bfloat16)
        for part in range(PARTS):
            shifts[part * width : (part + 1) * width, k * width : (k + 1) * width] = matrix


def shift_inline(value, shifts):
    largest = float(jnp.finfo(jnp.bfloat16).max)
    parts = []
    rest = value
    for part in range(PARTS):
        piece = (jnp.clip(rest, -largest, largest) if part == 0 else rest).astype(jnp.bfloat16)
        parts.append(piece)
        if part < PARTS - 1:
            rest = rest - piece.astype(jnp.float32)
    whole = jnp.concatenate(parts, axis=1)
    return jnp.dot(whole, shifts[...], preferred_element_type=jnp.float32)


def run_blocks(sizes, refs, slab, level_index, source, target, first_block, blocks):
    depth_count, line_count, _, row_count, freqs = sizes
    wide, shifts, bins_own, bins_other, shifted = refs
    line_index = lax.axis_index("xline")
    width = wide.shape[2]
    near_count = line_count // 2
    apart = slab ^ lax.axis_index("depth")
    slot = reversed_bits(apart, depth_count)
    odd = odd_bits(apart, depth_count)
    lane = lax.broadcasted_iota(jnp.int32, (SUB, width), 1)
    inside = {
        step: (lane + step >= 0) & (lane + step < width)
        for step in sorted(set(TAP_COLS) - {0} - set(STEPS))
    }
    top = pl.multiple_of(PAD + first_block * SUB, SUB)
    count = blocks * SUB
    rows = [source[array, pl.ds(top, count), :] for array in range(4 * freqs)]
    moved = shift_inline(jnp.concatenate(rows, axis=0), shifts)
    for array in range(4 * freqs):
        shifted[array, 0:count, :] = moved[array * count : (array + 1) * count]
    for block in range(blocks):
        row = pl.multiple_of((first_block + block) * SUB, SUB)
        line = (row // row_count) ^ line_index
        near = reversed_bits(line >> 1, near_count)
        inner = pl.multiple_of(row % row_count, SUB)
        own = bins_own[near, slot, level_index, pl.ds(inner, SUB), :]
        other = bins_other[near, slot, level_index, pl.ds(inner, SUB), :]
        crossed = odd ^ odd_bits(line >> 1, near_count)
        bins = jnp.where((line & 1) == crossed, own, other)
        for freq in range(freqs):
            sums = [None] * 4
            centre = None
            for tap in range(len(TAP_ROWS)):
                coefs = [
                    jnp.take_along_axis(
                        wide[(tap * 2 + part) * freqs + freq],
                        bins,
                        axis=1,
                        mode="promise_in_bounds",
                    )
                    for part in range(2)
                ]
                step = TAP_COLS[tap]
                if step == 0:
                    fields = [
                        source[kind * freqs + freq, pl.ds(PAD + row + TAP_ROWS[tap], SUB), :]
                        for kind in range(4)
                    ]
                    if tap == 0:
                        centre = fields
                elif step in STEPS:
                    lanes = pl.ds(STEPS.index(step) * width, width)
                    fields = [
                        shifted[kind * freqs + freq, pl.ds(block * SUB, SUB), lanes]
                        for kind in range(4)
                    ]
                else:
                    fields = [
                        jnp.where(inside[step], pltpu.roll(value, (-step) % width, 1), 0.0)
                        for value in centre
                    ]
                for field in range(2):
                    real, imag = fields[2 * field], fields[2 * field + 1]
                    term_real = coefs[0] * real - coefs[1] * imag
                    term_imag = coefs[0] * imag + coefs[1] * real
                    for part, term in ((0, term_real), (1, term_imag)):
                        place = 2 * field + part
                        sums[place] = term if sums[place] is None else sums[place] + term
            for kind in range(4):
                target[kind * freqs + freq, pl.ds(PAD + row, SUB), :] = sums[kind]


def run_slab(sizes, refs, slab, first, second, later=None):
    _, line_count, levels, row_count, _ = sizes
    grid_blocks = line_count * row_count // SUB
    chip_blocks = -(-2 * row_count // SUB)
    buffers = (first, second)
    for k in range(levels):
        run = functools.partial(
            run_blocks, sizes, refs, slab, k, buffers[k % 2], buffers[1 - k % 2]
        )
        blocks = grid_blocks
        first_block = 0
        if later is not None:
            reach = OFF_Y + REACH_ROWS * ((later + 1) * levels - 1 - k)
            margin = -(-reach // SUB)
            sides = 1 if line_count == 4 else 2
            blocks = min(grid_blocks, chip_blocks + sides * margin)
            chip = lax.axis_index("xline") >> 1
            first_block = jnp.clip(chip * chip_blocks - margin, 0, grid_blocks - blocks)

        def chunk_step(chunk, carry, run=run, first_block=first_block):
            run(first_block + chunk * CHUNK, CHUNK)
            return carry

        if blocks <= CHUNK:
            run(first_block, blocks)
        else:
            lax.fori_loop(0, blocks // CHUNK, chunk_step, 0)
            if blocks % CHUNK:
                run(first_block + blocks - blocks % CHUNK, blocks % CHUNK)
    if levels % 2:
        first[...] = second[...]


def continuation_kernel(
    sizes,
    table,
    offsets,
    surf_own,
    surf_other,
    bins_own,
    bins_other,
    mine,
    theirs,
    offsets_out,
    wide,
    shifts,
    shifted,
    first,
    second,
):
    _, line_count, _, row_count, freqs = sizes
    depth_index = lax.axis_index("depth")
    line_index = lax.axis_index("xline")
    near_count = line_count // 2
    parity = line_index & 1
    offsets_out[...] = offsets[...]
    for tap in range(len(TAP_ROWS)):
        for part in range(2):
            for freq in range(freqs):
                row = table[tap, part, pl.ds(parity * freqs + freq, 1), :]
                wide[(tap * 2 + part) * freqs + freq] = jnp.broadcast_to(row, wide.shape[1:])
    build_shifts(shifts, wide.shape[2])
    clear_edges(first)
    clear_edges(second)
    for near in range(near_count):
        odd = near.bit_count() & 1
        for own, source in ((odd, surf_own), (1 - odd, surf_other)):
            line = line_index ^ (2 * reversed_bits(near, near_count) + own)
            start = pl.multiple_of(PAD + line * row_count, SUB)
            for kind in range(4):
                for freq in range(freqs):
                    block = source[near, kind, parity * freqs + freq]
                    if kind == 3:
                        block = -block
                    first[kind * freqs + freq, pl.ds(start, row_count), :] = block
    refs = (wide, shifts, bins_own, bins_other, shifted)

    def slab_step(slab, carry, later=None):
        run_slab(sizes, refs, slab, first, second, later)
        return carry

    before_last = jnp.maximum(depth_index - 1, 0)
    lax.fori_loop(0, before_last, slab_step, 0)
    lax.fori_loop(before_last, depth_index, functools.partial(slab_step, later=1), 0)
    slab_step(depth_index, 0, later=0)
    tall = row_count + 2 * OFF_Y
    for out, line in ((mine, line_index), (theirs, line_index ^ 1)):
        base = pl.multiple_of(PAD + line * row_count, SUB)
        for array in range(2 * freqs):
            out[array * row_count : (array + 1) * row_count, :] = first[
                array, pl.ds(base, row_count), :
            ]
            below = 2 * freqs * row_count + array * tall
            above = pl.multiple_of(base - OFF_Y, SUB)
            out[below : below + tall, :] = first[2 * freqs + array, pl.ds(above, tall), :]


def image_kernel(freqs, offsets, mine, other, image):
    row_count, width = image.shape[2:]
    tall = row_count + 2 * OFF_Y
    lanes = lax.broadcasted_iota(jnp.int32, (row_count, width), 1)
    for h in range(image.shape[1]):
        dy = offsets[0, h]
        dx = offsets[1, h]
        valid = (lanes + dx >= 0) & (lanes + dx < width)
        total = None
        for pack in (mine, other):
            for array in range(2 * freqs):
                source = pack[array * row_count : (array + 1) * row_count, :]
                start = 2 * freqs * row_count + array * tall + OFF_Y
                value = pack[pl.ds(start + dy, row_count), :]
                term = source * pltpu.roll(value, lax.rem(width - dx, width), 1)
                if array >= freqs:
                    term = -term
                total = term if total is None else total + term
        image[0, h] = jnp.where(valid, total, 0.0)


def shards(surface_fields, stencil_table, velocity_bins, offset_list):
    depth_count = lax.axis_size("depth")
    line_count = lax.axis_size("xline")
    row_count = surface_fields.shape[3]
    width = surface_fields.shape[4]
    freqs = surface_fields.shape[2] // 2
    levels = velocity_bins.shape[1]
    grid_rows = row_count * line_count
    sizes = (depth_count, line_count, levels, row_count, freqs)
    depth_bits = bits_of(depth_count)
    line_bits = bits_of(line_count)[:-1]
    f32 = jnp.float32

    def call(kernel, outs, scratch, flops, *args):
        size = sum(array.size for array in (*args, *outs, *scratch))
        return pl.pallas_call(
            kernel,
            out_shape=outs,
            in_specs=[VMEM] * len(args),
            out_specs=[VMEM] * len(outs),
            scratch_shapes=[pltpu.VMEM(array.shape, array.dtype) for array in scratch],
            compiler_params=pltpu.CompilerParams(vmem_limit_bytes=4 * size + (2 << 20)),
            cost_estimate=pl.CostEstimate(flops=flops, bytes_accessed=4 * size, transcendentals=0),
        )(*args)

    like = jax.ShapeDtypeStruct
    surf = surface_fields.reshape(1, 4, 2 * freqs, row_count, width)
    (bins,) = call(
        load_kernel, [like(velocity_bins.shape, velocity_bins.dtype)], [], 1000, velocity_bins
    )

    top, below = depth_bits[:2]
    last, line = depth_bits[-1], line_bits[0]
    parts = [velocity_bins] + [
        hop(velocity_bins, bit, bit.bit_count() & 1)
        for bit in (top, top | below, below)
    ]
    parts[0] = bins
    bins = jnp.concatenate([parts[0], parts[1], parts[3], parts[2]], axis=0)
    surf = jnp.concatenate([surf, hop(surf, 0, line | 1)], axis=0)
    for bit in depth_bits[2:-1]:
        bins = jnp.concatenate([bins, hop(bins, bit, 1)], axis=0)
    depth_part = hop(bins, last, 1)
    line_part = hop(bins, 0, line | 1)
    cross_part = hop(bins, last, line)
    bins = jnp.stack(
        [
            jnp.concatenate([bins, depth_part], axis=0),
            jnp.concatenate([line_part, cross_part], axis=0),
        ]
    )
    for bit in line_bits[1:]:
        bins = jnp.concatenate([bins, hop(bins, 0, bit | 1)], axis=0)
        surf = jnp.concatenate([surf, hop(surf, 0, bit | 1)], axis=0)
    surf_other = hop(surf, 0, 1)
    bins_other = hop(bins, 0, 1)

    field_shape = (4 * freqs, grid_rows + 2 * PAD, width)
    field = like(field_shape, f32)
    work = depth_count * levels * len(TAP_ROWS) * 8 * field_shape[0] * grid_rows * width
    pack = like((2 * freqs * (2 * row_count + 2 * OFF_Y), width), f32)
    offsets = offset_list.T
    mine, theirs, offsets = call(
        functools.partial(continuation_kernel, sizes),
        [pack, pack, like(offsets.shape, offsets.dtype)],
        [
            like((len(TAP_ROWS) * 2 * freqs, SUB, width), f32),
            like((PARTS * width, len(STEPS) * width), jnp.bfloat16),
            like((4 * freqs, CHUNK * SUB, len(STEPS) * width), f32),
            field,
            field,
        ],
        work,
        stencil_table,
        offsets,
        surf,
        surf_other,
        bins,
        bins_other,
    )
    other = hop(theirs, 0, 1)
    image = pl.pallas_call(
        functools.partial(image_kernel, freqs),
        out_shape=like((1, offset_list.shape[0], row_count, width), f32),
        in_specs=[VMEM, VMEM, VMEM],
        out_specs=VMEM,
        compiler_params=pltpu.CompilerParams(vmem_limit_bytes=4 << 20),
        name="imaging",
    )(offsets, mine, other)
    return image


def solution(mesh):
    return jax.shard_map(
        shards,
        mesh=mesh,
        in_specs=(P(None, None, None, "xline", None), P(), P("depth", None, "xline", None), P()),
        out_specs=P("depth", None, "xline", None),
        check_vma=False,
    )
```

```python
import functools

import jax
import jax.numpy as jnp
from jax import lax
from jax.experimental import pallas as pl
from jax.experimental.pallas import tpu as pltpu
from jax.sharding import PartitionSpec as P

OFF_Y = 8
TAP_ROWS = (0, -4, -3, -2, -1, 1, 2, 3, 4, 0, 0, 0, 0)
TAP_COLS = (0, 0, 0, 0, 0, 0, 0, 0, 0, -2, -1, 1, 2)
PAD = 8
SUB = 8
CHUNK = 8
REACH_ROWS = 4
STEPS = (-2, -1, 1, 2)
PARTS = 2
VMEM = pl.BlockSpec(memory_space=pltpu.VMEM)


def bits_of(count):
    return [1 << k for k in reversed(range(count.bit_length() - 1))]


def reversed_bits(value, count):
    width = count.bit_length() - 1
    total = 0
    for k in range(width):
        total = total + (((value >> k) & 1) << (width - 1 - k))
    return total


def odd_bits(value, count):
    width = count.bit_length() - 1
    total = 0
    for k in range(width):
        total = total ^ ((value >> k) & 1)
    return total


def hop(block, depth_bit, line_bit):
    depths, lines = lax.axis_size("depth"), lax.axis_size("xline")
    route = [
        (d * lines + x, (d ^ depth_bit) * lines + (x ^ line_bit))
        for d in range(depths)
        for x in range(lines)
    ]
    return lax.ppermute(block, ("depth", "xline"), route)


def load_kernel(bins, bins_out):
    bins_out[...] = bins[...]


def clear_edges(buffer):
    count, rows, width = buffer.shape
    zeros = jnp.zeros((PAD, width), jnp.float32)
    for array in range(count):
        buffer[array, 0:PAD, :] = zeros
        buffer[array, rows - PAD : rows, :] = zeros


def build_shifts(shifts, width):
    source = lax.broadcasted_iota(jnp.int32, (width, width), 0)
    target = lax.broadcasted_iota(jnp.int32, (width, width), 1)
    for k, step in enumerate(STEPS):
        matrix = (source == target + step).astype(jnp.bfloat16)
        for part in range(PARTS):
            shifts[part * width : (part + 1) * width, k * width : (k + 1) * width] = matrix


def shift_inline(value, shifts):
    largest = float(jnp.finfo(jnp.bfloat16).max)
    parts = []
    rest = value
    for part in range(PARTS):
        piece = (jnp.clip(rest, -largest, largest) if part == 0 else rest).astype(jnp.bfloat16)
        parts.append(piece)
        if part < PARTS - 1:
            rest = rest - piece.astype(jnp.float32)
    whole = jnp.concatenate(parts, axis=1)
    return jnp.dot(whole, shifts[...], preferred_element_type=jnp.float32)


def run_blocks(sizes, refs, slab, level_index, source, target, first_block, blocks):
    depth_count, line_count, _, row_count, freqs = sizes
    wide, shifts, bins_own, bins_other, shifted = refs
    line_index = lax.axis_index("xline")
    width = wide.shape[2]
    near_count = line_count // 2
    apart = slab ^ lax.axis_index("depth")
    slot = reversed_bits(apart, depth_count)
    odd = odd_bits(apart, depth_count)
    lane = lax.broadcasted_iota(jnp.int32, (SUB, width), 1)
    inside = {
        step: (lane + step >= 0) & (lane + step < width)
        for step in sorted(set(TAP_COLS) - {0} - set(STEPS))
    }
    top = pl.multiple_of(PAD + first_block * SUB, SUB)
    count = blocks * SUB
    half = (blocks + 1) // 2 * SUB
    for low, high in ((0, half), (half, count)):
        size = high - low
        rows = [source[array, pl.ds(top + low, size), :] for array in range(4 * freqs)]
        moved = shift_inline(jnp.concatenate(rows, axis=0), shifts)
        for array in range(4 * freqs):
            shifted[array, low:high, :] = moved[array * size : (array + 1) * size]
    for block in range(blocks):
        row = pl.multiple_of((first_block + block) * SUB, SUB)
        line = (row // row_count) ^ line_index
        near = reversed_bits(line >> 1, near_count)
        inner = pl.multiple_of(row % row_count, SUB)
        own = bins_own[near, slot, level_index, pl.ds(inner, SUB), :]
        other = bins_other[near, slot, level_index, pl.ds(inner, SUB), :]
        crossed = odd ^ odd_bits(line >> 1, near_count)
        bins = jnp.where((line & 1) == crossed, own, other)
        for freq in range(freqs):
            sums = [None] * 4
            centre = None
            for tap in range(len(TAP_ROWS)):
                coefs = [
                    jnp.take_along_axis(
                        wide[(tap * 2 + part) * freqs + freq],
                        bins,
                        axis=1,
                        mode="promise_in_bounds",
                    )
                    for part in range(2)
                ]
                step = TAP_COLS[tap]
                if step == 0:
                    fields = [
                        source[kind * freqs + freq, pl.ds(PAD + row + TAP_ROWS[tap], SUB), :]
                        for kind in range(4)
                    ]
                    if tap == 0:
                        centre = fields
                elif step in STEPS:
                    lanes = pl.ds(STEPS.index(step) * width, width)
                    fields = [
                        shifted[kind * freqs + freq, pl.ds(block * SUB, SUB), lanes]
                        for kind in range(4)
                    ]
                else:
                    fields = [
                        jnp.where(inside[step], pltpu.roll(value, (-step) % width, 1), 0.0)
                        for value in centre
                    ]
                for field in range(2):
                    real, imag = fields[2 * field], fields[2 * field + 1]
                    term_real = coefs[0] * real - coefs[1] * imag
                    term_imag = coefs[0] * imag + coefs[1] * real
                    for part, term in ((0, term_real), (1, term_imag)):
                        place = 2 * field + part
                        sums[place] = term if sums[place] is None else sums[place] + term
            for kind in range(4):
                target[kind * freqs + freq, pl.ds(PAD + row, SUB), :] = sums[kind]


def run_slab(sizes, refs, slab, first, second, later=None):
    _, line_count, levels, row_count, _ = sizes
    grid_blocks = line_count * row_count // SUB
    chip_blocks = -(-2 * row_count // SUB)
    buffers = (first, second)
    for k in range(levels):
        run = functools.partial(
            run_blocks, sizes, refs, slab, k, buffers[k % 2], buffers[1 - k % 2]
        )
        blocks = grid_blocks
        first_block = 0
        if later is not None:
            reach = OFF_Y + REACH_ROWS * ((later + 1) * levels - 1 - k)
            margin = -(-reach // SUB)
            sides = 1 if line_count == 4 else 2
            blocks = min(grid_blocks, chip_blocks + sides * margin)
            chip = lax.axis_index("xline") >> 1
            first_block = jnp.clip(chip * chip_blocks - margin, 0, grid_blocks - blocks)

        def chunk_step(chunk, carry, run=run, first_block=first_block):
            run(first_block + chunk * CHUNK, CHUNK)
            return carry

        if blocks <= CHUNK:
            run(first_block, blocks)
        else:
            lax.fori_loop(0, blocks // CHUNK, chunk_step, 0)
            if blocks % CHUNK:
                run(first_block + blocks - blocks % CHUNK, blocks % CHUNK)
    if levels % 2:
        first[...] = second[...]


def continuation_kernel(
    sizes,
    table,
    offsets,
    surf_own,
    surf_other,
    bins_own,
    bins_other,
    mine,
    theirs,
    offsets_out,
    wide,
    shifts,
    shifted,
    first,
    second,
):
    _, line_count, _, row_count, freqs = sizes
    depth_index = lax.axis_index("depth")
    line_index = lax.axis_index("xline")
    near_count = line_count // 2
    parity = line_index & 1
    offsets_out[...] = offsets[...]
    for tap in range(len(TAP_ROWS)):
        for part in range(2):
            for freq in range(freqs):
                row = table[tap, part, pl.ds(parity * freqs + freq, 1), :]
                wide[(tap * 2 + part) * freqs + freq] = jnp.broadcast_to(row, wide.shape[1:])
    build_shifts(shifts, wide.shape[2])
    clear_edges(first)
    clear_edges(second)
    for near in range(near_count):
        odd = near.bit_count() & 1
        for own, source in ((odd, surf_own), (1 - odd, surf_other)):
            line = line_index ^ (2 * reversed_bits(near, near_count) + own)
            start = pl.multiple_of(PAD + line * row_count, SUB)
            for kind in range(4):
                for freq in range(freqs):
                    block = source[near, kind, parity * freqs + freq]
                    if kind == 3:
                        block = -block
                    first[kind * freqs + freq, pl.ds(start, row_count), :] = block
    refs = (wide, shifts, bins_own, bins_other, shifted)

    def slab_step(slab, carry, later=None):
        run_slab(sizes, refs, slab, first, second, later)
        return carry

    before_last = jnp.maximum(depth_index - 1, 0)
    lax.fori_loop(0, before_last, slab_step, 0)
    lax.fori_loop(before_last, depth_index, functools.partial(slab_step, later=1), 0)
    slab_step(depth_index, 0, later=0)
    tall = row_count + 2 * OFF_Y
    for out, line in ((mine, line_index), (theirs, line_index ^ 1)):
        base = pl.multiple_of(PAD + line * row_count, SUB)
        for array in range(2 * freqs):
            out[array * row_count : (array + 1) * row_count, :] = first[
                array, pl.ds(base, row_count), :
            ]
            below = 2 * freqs * row_count + array * tall
            above = pl.multiple_of(base - OFF_Y, SUB)
            out[below : below + tall, :] = first[2 * freqs + array, pl.ds(above, tall), :]


def image_kernel(freqs, offsets, mine, other, image):
    row_count, width = image.shape[2:]
    tall = row_count + 2 * OFF_Y
    lanes = lax.broadcasted_iota(jnp.int32, (row_count, width), 1)
    for h in range(image.shape[1]):
        dy = offsets[0, h]
        dx = offsets[1, h]
        valid = (lanes + dx >= 0) & (lanes + dx < width)
        total = None
        for pack in (mine, other):
            for array in range(2 * freqs):
                source = pack[array * row_count : (array + 1) * row_count, :]
                start = 2 * freqs * row_count + array * tall + OFF_Y
                value = pack[pl.ds(start + dy, row_count), :]
                term = source * pltpu.roll(value, lax.rem(width - dx, width), 1)
                if array >= freqs:
                    term = -term
                total = term if total is None else total + term
        image[0, h] = jnp.where(valid, total, 0.0)


def shards(surface_fields, stencil_table, velocity_bins, offset_list):
    depth_count = lax.axis_size("depth")
    line_count = lax.axis_size("xline")
    row_count = surface_fields.shape[3]
    width = surface_fields.shape[4]
    freqs = surface_fields.shape[2] // 2
    levels = velocity_bins.shape[1]
    grid_rows = row_count * line_count
    sizes = (depth_count, line_count, levels, row_count, freqs)
    depth_bits = bits_of(depth_count)
    line_bits = bits_of(line_count)[:-1]
    f32 = jnp.float32

    def call(kernel, outs, scratch, flops, *args):
        size = sum(array.size for array in (*args, *outs, *scratch))
        return pl.pallas_call(
            kernel,
            out_shape=outs,
            in_specs=[VMEM] * len(args),
            out_specs=[VMEM] * len(outs),
            scratch_shapes=[pltpu.VMEM(array.shape, array.dtype) for array in scratch],
            compiler_params=pltpu.CompilerParams(vmem_limit_bytes=4 * size + (2 << 20)),
            cost_estimate=pl.CostEstimate(flops=flops, bytes_accessed=4 * size, transcendentals=0),
        )(*args)

    like = jax.ShapeDtypeStruct
    surf = surface_fields.reshape(1, 4, 2 * freqs, row_count, width)
    (bins,) = call(
        load_kernel, [like(velocity_bins.shape, velocity_bins.dtype)], [], 1000, velocity_bins
    )

    top, below = depth_bits[:2]
    last, line = depth_bits[-1], line_bits[0]
    parts = [velocity_bins] + [
        hop(velocity_bins, bit, bit.bit_count() & 1)
        for bit in (top, top | below, below)
    ]
    parts[0] = bins
    bins = jnp.concatenate([parts[0], parts[1], parts[3], parts[2]], axis=0)
    surf = jnp.concatenate([surf, hop(surf, 0, line | 1)], axis=0)
    for bit in depth_bits[2:-1]:
        bins = jnp.concatenate([bins, hop(bins, bit, 1)], axis=0)
    depth_part = hop(bins, last, 1)
    line_part = hop(bins, 0, line | 1)
    cross_part = hop(bins, last, line)
    bins = jnp.stack(
        [
            jnp.concatenate([bins, depth_part], axis=0),
            jnp.concatenate([line_part, cross_part], axis=0),
        ]
    )
    for bit in line_bits[1:]:
        bins = jnp.concatenate([bins, hop(bins, 0, bit | 1)], axis=0)
        surf = jnp.concatenate([surf, hop(surf, 0, bit | 1)], axis=0)
    surf_other = hop(surf, 0, 1)
    bins_other = hop(bins, 0, 1)

    field_shape = (4 * freqs, grid_rows + 2 * PAD, width)
    field = like(field_shape, f32)
    work = depth_count * levels * len(TAP_ROWS) * 8 * field_shape[0] * grid_rows * width
    pack = like((2 * freqs * (2 * row_count + 2 * OFF_Y), width), f32)
    offsets = offset_list.T
    mine, theirs, offsets = call(
        functools.partial(continuation_kernel, sizes),
        [pack, pack, like(offsets.shape, offsets.dtype)],
        [
            like((len(TAP_ROWS) * 2 * freqs, SUB, width), f32),
            like((PARTS * width, len(STEPS) * width), jnp.bfloat16),
            like((4 * freqs, CHUNK * SUB, len(STEPS) * width), f32),
            field,
            field,
        ],
        work,
        stencil_table,
        offsets,
        surf,
        surf_other,
        bins,
        bins_other,
    )
    other = hop(theirs, 0, 1)
    image = pl.pallas_call(
        functools.partial(image_kernel, freqs),
        out_shape=like((1, offset_list.shape[0], row_count, width), f32),
        in_specs=[VMEM, VMEM, VMEM],
        out_specs=VMEM,
        compiler_params=pltpu.CompilerParams(vmem_limit_bytes=4 << 20),
        name="imaging",
    )(offsets, mine, other)
    return image


def solution(mesh):
    return jax.shard_map(
        shards,
        mesh=mesh,
        in_specs=(P(None, None, None, "xline", None), P(), P("depth", None, "xline", None), P()),
        out_specs=P("depth", None, "xline", None),
        check_vma=False,
    )
```

```python
import functools

import jax
import jax.numpy as jnp
from jax import lax
from jax.experimental import pallas as pl
from jax.experimental.pallas import tpu as pltpu
from jax.sharding import PartitionSpec as P

OFF_Y = 8
TAP_ROWS = (0, -4, -3, -2, -1, 1, 2, 3, 4, 0, 0, 0, 0)
TAP_COLS = (0, 0, 0, 0, 0, 0, 0, 0, 0, -2, -1, 1, 2)
PAD = 8
SUB = 8
CHUNK = 8
REACH_ROWS = 4
STEPS = (-2, -1, 1, 2)
PARTS = 2
VMEM = pl.BlockSpec(memory_space=pltpu.VMEM)


def bits_of(count):
    return [1 << k for k in reversed(range(count.bit_length() - 1))]


def reversed_bits(value, count):
    width = count.bit_length() - 1
    total = 0
    for k in range(width):
        total = total + (((value >> k) & 1) << (width - 1 - k))
    return total


def odd_bits(value, count):
    width = count.bit_length() - 1
    total = 0
    for k in range(width):
        total = total ^ ((value >> k) & 1)
    return total


def hop(block, depth_bit, line_bit):
    depths, lines = lax.axis_size("depth"), lax.axis_size("xline")
    route = [
        (d * lines + x, (d ^ depth_bit) * lines + (x ^ line_bit))
        for d in range(depths)
        for x in range(lines)
    ]
    return lax.ppermute(block, ("depth", "xline"), route)


def load_kernel(bins, bins_out):
    bins_out[...] = bins[...]


def clear_edges(buffer):
    count, rows, width = buffer.shape
    zeros = jnp.zeros((PAD, width), jnp.float32)
    for array in range(count):
        buffer[array, 0:PAD, :] = zeros
        buffer[array, rows - PAD : rows, :] = zeros


def build_shifts(shifts, width):
    source = lax.broadcasted_iota(jnp.int32, (width, width), 0)
    target = lax.broadcasted_iota(jnp.int32, (width, width), 1)
    for k, step in enumerate(STEPS):
        matrix = (source == target + step).astype(jnp.bfloat16)
        for part in range(PARTS):
            shifts[part * width : (part + 1) * width, k * width : (k + 1) * width] = matrix


def shift_inline(value, shifts):
    largest = float(jnp.finfo(jnp.bfloat16).max)
    parts = []
    rest = value
    for part in range(PARTS):
        piece = (jnp.clip(rest, -largest, largest) if part == 0 else rest).astype(jnp.bfloat16)
        parts.append(piece)
        if part < PARTS - 1:
            rest = rest - piece.astype(jnp.float32)
    whole = jnp.concatenate(parts, axis=1)
    return jnp.dot(whole, shifts[...], preferred_element_type=jnp.float32)


def run_blocks(sizes, refs, slab, level_index, source, target, first_block, blocks):
    depth_count, line_count, _, row_count, freqs = sizes
    wide, shifts, bins_own, bins_other, shifted = refs
    line_index = lax.axis_index("xline")
    width = wide.shape[2]
    near_count = line_count // 2
    apart = slab ^ lax.axis_index("depth")
    slot = reversed_bits(apart, depth_count)
    odd = odd_bits(apart, depth_count)
    lane = lax.broadcasted_iota(jnp.int32, (SUB, width), 1)
    inside = {
        step: (lane + step >= 0) & (lane + step < width)
        for step in sorted(set(TAP_COLS) - {0} - set(STEPS))
    }
    top = pl.multiple_of(PAD + first_block * SUB, SUB)
    count = blocks * SUB
    half = (blocks + 1) // 2 * SUB
    for low, high in ((0, half), (half, count)):
        size = high - low
        rows = [source[array, pl.ds(top + low, size), :] for array in range(4 * freqs)]
        moved = shift_inline(jnp.concatenate(rows, axis=0), shifts)
        for array in range(4 * freqs):
            shifted[array, low:high, :] = moved[array * size : (array + 1) * size]
    for block in range(blocks):
        row = pl.multiple_of((first_block + block) * SUB, SUB)
        line = (row // row_count) ^ line_index
        near = reversed_bits(line >> 1, near_count)
        inner = pl.multiple_of(row % row_count, SUB)
        own = bins_own[near, slot, level_index, pl.ds(inner, SUB), :]
        other = bins_other[near, slot, level_index, pl.ds(inner, SUB), :]
        crossed = odd ^ odd_bits(line >> 1, near_count)
        bins = jnp.where((line & 1) == crossed, own, other)
        for freq in range(freqs):
            sums = [None] * 4
            centre = None
            for tap in range(len(TAP_ROWS)):
                coefs = [
                    jnp.take_along_axis(
                        wide[(tap * 2 + part) * freqs + freq],
                        bins,
                        axis=1,
                        mode="promise_in_bounds",
                    )
                    for part in range(2)
                ]
                step = TAP_COLS[tap]
                if step == 0:
                    fields = [
                        source[kind * freqs + freq, pl.ds(PAD + row + TAP_ROWS[tap], SUB), :]
                        for kind in range(4)
                    ]
                    if tap == 0:
                        centre = fields
                elif step in STEPS:
                    lanes = pl.ds(STEPS.index(step) * width, width)
                    fields = [
                        shifted[kind * freqs + freq, pl.ds(block * SUB, SUB), lanes]
                        for kind in range(4)
                    ]
                else:
                    fields = [
                        jnp.where(inside[step], pltpu.roll(value, (-step) % width, 1), 0.0)
                        for value in centre
                    ]
                for field in range(2):
                    real, imag = fields[2 * field], fields[2 * field + 1]
                    term_real = coefs[0] * real - coefs[1] * imag
                    term_imag = coefs[0] * imag + coefs[1] * real
                    for part, term in ((0, term_real), (1, term_imag)):
                        place = 2 * field + part
                        sums[place] = term if sums[place] is None else sums[place] + term
            for kind in range(4):
                target[kind * freqs + freq, pl.ds(PAD + row, SUB), :] = sums[kind]


def run_slab(sizes, refs, slab, first, second, later=None):
    _, line_count, levels, row_count, _ = sizes
    grid_blocks = line_count * row_count // SUB
    chip_blocks = -(-2 * row_count // SUB)
    buffers = (first, second)
    for k in range(levels):
        run = functools.partial(
            run_blocks, sizes, refs, slab, k, buffers[k % 2], buffers[1 - k % 2]
        )
        blocks = grid_blocks
        first_block = 0
        if later is not None:
            reach = OFF_Y + REACH_ROWS * ((later + 1) * levels - 1 - k)
            margin = -(-reach // SUB)
            sides = 1 if line_count == 4 else 2
            blocks = min(grid_blocks, chip_blocks + sides * margin)
            chip = lax.axis_index("xline") >> 1
            first_block = jnp.clip(chip * chip_blocks - margin, 0, grid_blocks - blocks)

        def chunk_step(chunk, carry, run=run, first_block=first_block):
            run(first_block + chunk * CHUNK, CHUNK)
            return carry

        if blocks <= CHUNK:
            run(first_block, blocks)
        else:
            lax.fori_loop(0, blocks // CHUNK, chunk_step, 0)
            if blocks % CHUNK:
                run(first_block + blocks - blocks % CHUNK, blocks % CHUNK)
    if levels % 2:
        first[...] = second[...]


def continuation_kernel(
    sizes,
    table,
    offsets,
    surf_own,
    surf_other,
    bins_own,
    bins_other,
    mine,
    theirs,
    offsets_out,
    wide,
    shifts,
    shifted,
    first,
    second,
):
    _, line_count, _, row_count, freqs = sizes
    depth_index = lax.axis_index("depth")
    line_index = lax.axis_index("xline")
    near_count = line_count // 2
    parity = line_index & 1
    offsets_out[...] = offsets[...]
    for tap in range(len(TAP_ROWS)):
        for part in range(2):
            for freq in range(freqs):
                row = table[tap, part, pl.ds(parity * freqs + freq, 1), :]
                wide[(tap * 2 + part) * freqs + freq] = jnp.broadcast_to(row, wide.shape[1:])
    build_shifts(shifts, wide.shape[2])
    clear_edges(first)
    clear_edges(second)
    for near in range(near_count):
        odd = near.bit_count() & 1
        for own, source in ((odd, surf_own), (1 - odd, surf_other)):
            line = line_index ^ (2 * reversed_bits(near, near_count) + own)
            start = pl.multiple_of(PAD + line * row_count, SUB)
            for kind in range(4):
                for freq in range(freqs):
                    block = source[near, kind, parity * freqs + freq]
                    if kind == 3:
                        block = -block
                    first[kind * freqs + freq, pl.ds(start, row_count), :] = block
    refs = (wide, shifts, bins_own, bins_other, shifted)

    def slab_step(slab, carry, later=None):
        run_slab(sizes, refs, slab, first, second, later)
        return carry

    before_last = jnp.maximum(depth_index - 1, 0)
    lax.fori_loop(0, before_last, slab_step, 0)
    lax.fori_loop(before_last, depth_index, functools.partial(slab_step, later=1), 0)
    slab_step(depth_index, 0, later=0)
    tall = row_count + 2 * OFF_Y
    for out, line in ((mine, line_index), (theirs, line_index ^ 1)):
        base = pl.multiple_of(PAD + line * row_count, SUB)
        for array in range(2 * freqs):
            out[array * row_count : (array + 1) * row_count, :] = first[
                array, pl.ds(base, row_count), :
            ]
            below = 2 * freqs * row_count + array * tall
            above = pl.multiple_of(base - OFF_Y, SUB)
            out[below : below + tall, :] = first[2 * freqs + array, pl.ds(above, tall), :]


def image_kernel(freqs, offsets, pack, *images):
    image = images[-1]
    row_count, width = image.shape[2:]
    tall = row_count + 2 * OFF_Y
    lanes = lax.broadcasted_iota(jnp.int32, (row_count, width), 1)
    for h in range(image.shape[1]):
        dy = offsets[0, h]
        dx = offsets[1, h]
        valid = (lanes + dx >= 0) & (lanes + dx < width)
        total = None
        for array in range(2 * freqs):
            source = pack[array * row_count : (array + 1) * row_count, :]
            start = 2 * freqs * row_count + array * tall + OFF_Y
            value = pack[pl.ds(start + dy, row_count), :]
            term = source * pltpu.roll(value, lax.rem(width - dx, width), 1)
            if array >= freqs:
                term = -term
            total = term if total is None else total + term
        total = jnp.where(valid, total, 0.0)
        image[0, h] = total if len(images) == 1 else images[0][0, h] + total


def shards(surface_fields, stencil_table, velocity_bins, offset_list):
    depth_count = lax.axis_size("depth")
    line_count = lax.axis_size("xline")
    row_count = surface_fields.shape[3]
    width = surface_fields.shape[4]
    freqs = surface_fields.shape[2] // 2
    levels = velocity_bins.shape[1]
    grid_rows = row_count * line_count
    sizes = (depth_count, line_count, levels, row_count, freqs)
    depth_bits = bits_of(depth_count)
    line_bits = bits_of(line_count)[:-1]
    f32 = jnp.float32

    def call(kernel, outs, scratch, flops, *args):
        size = sum(array.size for array in (*args, *outs, *scratch))
        return pl.pallas_call(
            kernel,
            out_shape=outs,
            in_specs=[VMEM] * len(args),
            out_specs=[VMEM] * len(outs),
            scratch_shapes=[pltpu.VMEM(array.shape, array.dtype) for array in scratch],
            compiler_params=pltpu.CompilerParams(vmem_limit_bytes=4 * size + (2 << 20)),
            cost_estimate=pl.CostEstimate(flops=flops, bytes_accessed=4 * size, transcendentals=0),
        )(*args)

    like = jax.ShapeDtypeStruct
    surf = surface_fields.reshape(1, 4, 2 * freqs, row_count, width)
    (bins,) = call(
        load_kernel, [like(velocity_bins.shape, velocity_bins.dtype)], [], 1000, velocity_bins
    )

    top, below = depth_bits[:2]
    last, line = depth_bits[-1], line_bits[0]
    parts = [velocity_bins] + [
        hop(velocity_bins, bit, bit.bit_count() & 1)
        for bit in (top, top | below, below)
    ]
    parts[0] = bins
    bins = jnp.concatenate([parts[0], parts[1], parts[3], parts[2]], axis=0)
    surf = jnp.concatenate([surf, hop(surf, 0, line | 1)], axis=0)
    for bit in depth_bits[2:-1]:
        bins = jnp.concatenate([bins, hop(bins, bit, 1)], axis=0)
    depth_part = hop(bins, last, 1)
    line_part = hop(bins, 0, line | 1)
    cross_part = hop(bins, last, line)
    bins = jnp.stack(
        [
            jnp.concatenate([bins, depth_part], axis=0),
            jnp.concatenate([line_part, cross_part], axis=0),
        ]
    )
    for bit in line_bits[1:]:
        bins = jnp.concatenate([bins, hop(bins, 0, bit | 1)], axis=0)
        surf = jnp.concatenate([surf, hop(surf, 0, bit | 1)], axis=0)
    surf_other = hop(surf, 0, 1)
    bins_other = hop(bins, 0, 1)

    field_shape = (4 * freqs, grid_rows + 2 * PAD, width)
    field = like(field_shape, f32)
    work = depth_count * levels * len(TAP_ROWS) * 8 * field_shape[0] * grid_rows * width
    pack = like((2 * freqs * (2 * row_count + 2 * OFF_Y), width), f32)
    offsets = offset_list.T
    mine, theirs, offsets = call(
        functools.partial(continuation_kernel, sizes),
        [pack, pack, like(offsets.shape, offsets.dtype)],
        [
            like((len(TAP_ROWS) * 2 * freqs, SUB, width), f32),
            like((PARTS * width, len(STEPS) * width), jnp.bfloat16),
            like((4 * freqs, CHUNK * SUB, len(STEPS) * width), f32),
            field,
            field,
        ],
        work,
        stencil_table,
        offsets,
        surf,
        surf_other,
        bins,
        bins_other,
    )
    other = hop(theirs, 0, 1)
    shape = like((1, offset_list.shape[0], row_count, width), f32)
    imaging = functools.partial(image_kernel, freqs)
    (partial,) = call(imaging, [shape], [], 1000, offsets, mine)
    (image,) = call(imaging, [shape], [], 1000, offsets, other, partial)
    return image


def solution(mesh):
    return jax.shard_map(
        shards,
        mesh=mesh,
        in_specs=(P(None, None, None, "xline", None), P(), P("depth", None, "xline", None), P()),
        out_specs=P("depth", None, "xline", None),
        check_vma=False,
    )
```
